512 devices in a mesh: ep: 32 (over y, x), tp: 16 (over z, core).
Axes of the slice: x: 4, y: 8, z: 8, core: 2. Of those that a mesh axis runs over, the one named last changes fastest.
Arguments:
- quantized: bfloat16 [32, 4096, 2048], P('ep', None, 'tp'), may hold values from -4 to 4
- block_scale: bfloat16 [32, 32, 16], P('ep', None, 'tp'), may hold values from 0.01 to 1
- slot_expert: int32 [64], replicated, may hold values from 0 to 31, as said below
Outputs:
- serving: bfloat16 [64, 4096, 2048], P('ep', None, 'tp')
- tensor_scale: float32 [64], P('ep')
The draws below stay inside these ranges and needn't reach their ends.
Inputs may be any that keep to these rules, and one draw needn't show every extreme that they name: `slot_expert`: slot j belongs to the holder of index j // 2 of ep; every expert has at least one slot, and an expert may have several.
All inputs are finite; a program needn't handle non-finite values. Where the reference program divides by a largest or mean magnitude, that divisor is 1e-20 or more.
Results may differ from the reference program's by a relative error of at most 0.001.
Values may be sent and summed in bfloat16 or wider, within the bound.
A program may use at most 64 MiB of HBM per device.

```python
import math
import jax
import jax.numpy as jnp
from jax import lax

BLOCK = 128
ROWS = 4096
COLS = 2048
EXPERTS = 32
SLOTS_TOTAL = 64


def draw_block_scale(key, part):
    uniform_vals = jax.random.uniform(key, (EXPERTS, ROWS // BLOCK, COLS // BLOCK), jnp.float32, 0.001, 1.0)
    scales = 0.01 * uniform_vals ** (-0.5)
    return jnp.clip(scales, 0.01, 1.0).astype(jnp.bfloat16)


def draw_slot_expert(key, part):
    first_key = jax.random.fold_in(key, 11)
    second_key = jax.random.fold_in(key, 23)
    third_key = jax.random.fold_in(key, 37)
    extra_count = SLOTS_TOTAL - EXPERTS
    picks = jax.random.randint(first_key, (4, extra_count), 0, EXPERTS, jnp.int32)
    ranked = jnp.min(picks, axis=0)
    relabel = jax.random.permutation(second_key, jnp.arange(EXPERTS, dtype=jnp.int32))
    extras = jnp.take(relabel, ranked, axis=0)
    copies = jnp.concatenate([jnp.arange(EXPERTS, dtype=jnp.int32), extras])
    order = jax.random.permutation(third_key, jnp.arange(SLOTS_TOTAL, dtype=jnp.int32))
    return jnp.take(copies, order, axis=0).astype(jnp.int32)


def levels(own_key, extent, cuts, least, top_value):
    level, own = 1.0, jax.random.fold_in(own_key, 6)
    for axis_at, parts in cuts:
        draws = jnp.exp(jax.random.uniform(jax.random.fold_in(own, axis_at), (parts,), jnp.float32, least / len(cuts), top_value / len(cuts)))
        level = level * jnp.repeat(draws, extent[axis_at] // parts).reshape([-1 if axis == axis_at else 1 for axis in range(len(extent))])
    return level


def noise(stream_key, extent, scale, limit, cuts=(), kind=jnp.bfloat16):
    entries = jax.random.normal(stream_key, extent, jnp.float32) * scale
    if len(cuts) > 0:
        entries = levels(stream_key, extent, cuts, -0.22, 0.18) * entries
    return jnp.clip(entries, min=-limit, max=limit).astype(kind)


def setup_inputs(seed: int = 0) -> dict:
    splits = jax.random.split(jax.random.key(seed), 4)
    return {
        "quantized": noise(splits[0], (EXPERTS, ROWS, COLS), 1.0, 4.0, ((0, 32), (2, 16))),
        "block_scale": draw_block_scale(jax.random.fold_in(splits[3], 71), 0),
        "slot_expert": draw_slot_expert(jax.random.fold_in(splits[3], 71), 0),
    }


EPSILON = 1e-06

def hadamard(length):
    indices = jnp.arange(length, dtype=jnp.int32)
    common = indices[:, None] & indices[None, :]
    parity = jnp.zeros((length, length), jnp.int32)
    for position in range(length.bit_length() - 1):
        parity = parity + (common >> position & 1)
    return (1 - 2 * (parity % 2)).astype(jnp.float32) / math.sqrt(length)

def one_expert(pieces):
    values, scales = pieces
    row_count, col_count = values.shape
    blocks = values.astype(jnp.float32).reshape(row_count // BLOCK, BLOCK, col_count // BLOCK, BLOCK)
    blocks = blocks * scales.astype(jnp.float32)[:, None, :, None]
    rotated = jnp.einsum('iajb,bc->iajc', blocks, hadamard(BLOCK), precision=lax.Precision.HIGHEST)
    largest = jnp.max(jnp.abs(rotated))
    unit_vals = (rotated / (largest + EPSILON)).reshape(row_count, col_count).astype(jnp.bfloat16)
    return (unit_vals, largest)

def reference(quantized, block_scale, slot_expert):
    units, amaxes = lax.map(one_expert, (quantized, block_scale))
    serving = jnp.take(units, slot_expert.astype(jnp.int32), axis=0)
    tensor_scale = jnp.take(amaxes, slot_expert.astype(jnp.int32), axis=0)
    return (serving, tensor_scale)
```

```python
import functools
import math

import jax
import jax.numpy as jnp
from jax import lax
from jax.experimental import pallas as pl
from jax.experimental.pallas import tpu as pltpu
from jax.sharding import PartitionSpec as P

MESH = pl.DeviceIdType.MESH
BLOCK = 128
EPSILON = 1e-06
NX, NY = 4, 8
EP = NX * NY
REACH = 4
STAGES = 4
PIECE = BLOCK // STAGES
HALF = REACH * NX


def sign_matrix():
    rows = lax.broadcasted_iota(jnp.int32, (BLOCK, BLOCK), 0)
    cols = lax.broadcasted_iota(jnp.int32, (BLOCK, BLOCK), 1)
    common = rows & cols
    common = common ^ (common >> 4)
    common = common ^ (common >> 2)
    common = common ^ (common >> 1)
    return (1 - 2 * (common & 1)).astype(jnp.float32).astype(jnp.bfloat16)


def to_column(row, count):
    spread = jnp.broadcast_to(row, (count, BLOCK))
    at_row = lax.broadcasted_iota(jnp.int32, (count, BLOCK), 0)
    at_lane = lax.broadcasted_iota(jnp.int32, (count, BLOCK), 1)
    return jnp.sum(jnp.where(at_row == at_lane, spread, 0.0), axis=1, keepdims=True)


def move_kernel(
    tp_bits,
    slot_ref,
    stored_ref,
    scale_ref,
    raw_ref,
    table_ref,
    own,
    signs,
    picked,
    block_max,
    peer_out,
    peer_in,
    row_out,
    own_sem,
    near_sem,
    far_sem,
    in_sem,
    row_sem,
    peer_sem,
    send_near,
    send_far,
    send_in,
    send_row,
    send_peer,
    *held_refs,
):
    held = (held_refs[:STAGES], held_refs[STAGES:])
    me = lax.axis_index("ep")
    tp = lax.axis_index("tp")
    here_y, here_x = me // NX, lax.rem(me, NX)
    row_blocks = stored_ref.shape[0] // BLOCK

    barrier = pltpu.get_barrier_semaphore()

    def greet(step, _):
        pl.semaphore_signal(
            barrier, inc=1, device_id=(lax.rem(me + step, EP), tp), device_id_type=MESH
        )
        return _

    lax.fori_loop(1, EP, greet, 0)
    for bit in range(tp_bits):
        pl.semaphore_signal(
            barrier, inc=1, device_id=(me, tp ^ (1 << bit)), device_id_type=MESH
        )
    pl.semaphore_wait(barrier, EP - 1 + tp_bits)

    own_copy = pltpu.make_async_copy(stored_ref, own, own_sem)

    def near_rows(side, reach, stage):
        to_y = lax.rem(here_y + (NY + reach if side == 0 else NY - reach), NY)
        chunk = lax.rem(to_y + NY - side, NY)
        return to_y, chunk

    def near_copy(side, reach, dx, stage):
        to_y, chunk = near_rows(side, reach, stage)
        to_x = lax.rem(here_x + dx, NX)
        start = pl.multiple_of((chunk * NX + to_x) * BLOCK + stage * PIECE, PIECE)
        return (
            stored_ref.at[pl.ds(start, PIECE)],
            held[side][stage].at[reach * NX + here_x],
            (to_y * NX + to_x, tp),
        )

    for stage in range(STAGES):
        for side in range(2):
            source, target, _ = near_copy(side, 0, 0, stage)
            pltpu.make_async_copy(source, target, near_sem.at[side, stage]).start()

        def send_one(step, _, stage=stage):
            for side in range(2):
                source, target, device = near_copy(side, step // NX, lax.rem(step, NX), stage)
                pltpu.make_async_remote_copy(
                    src_ref=source,
                    dst_ref=target,
                    send_sem=send_near,
                    recv_sem=near_sem.at[side, stage],
                    device_id=device,
                    device_id_type=MESH,
                ).start()
            return _

        lax.fori_loop(1, HALF, send_one, 0)

    own_copy.start()
    signs[...] = sign_matrix()
    own_copy.wait()

    def one_block(index, _):
        rows = own[pl.ds(pl.multiple_of(index * BLOCK, BLOCK), BLOCK), :]
        turned = jnp.dot(rows, signs[...], preferred_element_type=jnp.float32)
        block_max[pl.ds(index, 1), :] = jnp.max(jnp.abs(turned), axis=0, keepdims=True)
        return _

    lax.fori_loop(0, row_blocks, one_block, 0)

    row_out[...] = jnp.zeros_like(row_out)
    row_out[0, :, 0:row_blocks] = scale_ref[...].astype(jnp.float32)
    scale_row = row_out[0, :, :]
    largest = jnp.max(block_max[...] * to_column(scale_row, row_blocks)) * (1.0 / math.sqrt(BLOCK))

    def peer_copy(bit):
        return pltpu.make_async_remote_copy(
            src_ref=peer_out.at[bit],
            dst_ref=peer_in.at[bit],
            send_sem=send_peer.at[bit],
            recv_sem=peer_sem.at[bit],
            device_id=(me, tp ^ (1 << bit)),
            device_id_type=MESH,
        )

    def peer_start(bit, value):
        peer_out[bit] = value
        peer_copy(bit).start()

    def peer_finish(bit):
        peer_copy(bit).wait()
        return jnp.maximum(peer_out[bit], peer_in[bit])

    state = {"value": jnp.full((8, BLOCK), largest, jnp.float32), "bit": 0}

    def row_copy(step):
        return pltpu.make_async_remote_copy(
            src_ref=row_out.at[0],
            dst_ref=table_ref.at[me],
            send_sem=send_row,
            recv_sem=row_sem,
            device_id=(lax.rem(me + step, EP), tp),
            device_id_type=MESH,
        )

    def send_rows(value):
        lane = lax.broadcasted_iota(jnp.int32, (1, BLOCK), 1)
        row_out[0, :, :] = jnp.where(lane < row_blocks, scale_row, value[0:1, :])
        pltpu.make_async_copy(row_out.at[0], table_ref.at[me], row_sem).start()

        def send_row_to(step, _):
            row_copy(step).start()
            return _

        lax.fori_loop(1, EP, send_row_to, 0)

    def advance():
        bit = state["bit"]
        if bit > 0 and bit <= tp_bits:
            state["value"] = peer_finish(bit - 1)
        if bit < tp_bits:
            peer_start(bit, state["value"])
        if bit == tp_bits:
            send_rows(state["value"])
        state["bit"] = bit + 1

    def far_copy(side, stage):
        to_y = lax.rem(here_y + (1 if side == 0 else NY - 1), NY)
        return pltpu.make_async_remote_copy(
            src_ref=held[side][stage].at[pl.ds(0, HALF)],
            dst_ref=held[1 - side][stage].at[pl.ds(HALF, HALF)],
            send_sem=send_far,
            recv_sem=far_sem.at[1 - side, stage],
            device_id=(to_y * NX + here_x, tp),
            device_id_type=MESH,
        )

    advance()
    for stage in range(STAGES):
        for side in range(2):
            arrived = held[side][stage].at[pl.ds(0, HALF)]
            pltpu.make_async_copy(arrived, arrived, near_sem.at[side, stage]).wait()
            far_copy(side, stage).start()
        advance()

    def in_target(side, step, stage):
        reach, dx = step // NX, lax.rem(step, NX)
        to_y = lax.rem(here_y + (NY - reach if side == 0 else NY + reach), NY)
        return to_y * NX + lax.rem(here_x + dx, NX)

    def in_rows(side, stage):
        chunk = lax.rem(here_y + NY - side, NY)
        start = pl.multiple_of((chunk * NX + here_x) * BLOCK + stage * PIECE, PIECE)
        return raw_ref.at[:, pl.ds(start, PIECE)]

    for stage in range(STAGES):
        for side in range(2):
            arrived = held[side][stage].at[pl.ds(HALF, HALF)]
            pltpu.make_async_copy(arrived, arrived, far_sem.at[side, stage]).wait()

            def pick(step, _, side=side, stage=stage):
                device = in_target(side, step, stage)
                for slot in range(2):
                    expert = slot_ref[2 * device + slot]
                    from_y, from_x = expert >> 2, expert & 3
                    away = (here_y - from_y if side == 0 else from_y - here_y) & 7
                    index = jnp.where(away < REACH, away, HALF // NX + 7 - away) * NX + from_x
                    picked[stage, side * HALF + step, slot] = held[side][stage][index]
                return _

            lax.fori_loop(0, HALF, pick, 0)

            local = picked.at[stage, side * HALF]
            pltpu.make_async_copy(local, in_rows(side, stage), in_sem.at[stage]).start()

            def send_in_one(step, _, side=side, stage=stage):
                pltpu.make_async_remote_copy(
                    src_ref=picked.at[stage, side * HALF + step],
                    dst_ref=in_rows(side, stage),
                    send_sem=send_in,
                    recv_sem=in_sem.at[stage],
                    device_id=(in_target(side, step, stage), tp),
                    device_id_type=MESH,
                ).start()
                return _

            lax.fori_loop(1, HALF, send_in_one, 0)
        advance()

    while state["bit"] <= tp_bits:
        advance()

    pltpu.make_async_copy(table_ref, table_ref, row_sem).wait()
    for stage in range(STAGES):
        part = raw_ref.at[:, pl.ds(0, EP * PIECE)]
        pltpu.make_async_copy(part, part, in_sem.at[stage]).wait()
    sent = table_ref.at[pl.ds(0, EP - 1)]
    pltpu.make_async_copy(sent, sent, send_row).wait()
    sent = own.at[pl.ds(0, 2 * (HALF - 1) * BLOCK)]
    pltpu.make_async_copy(sent, sent, send_near).wait()
    sent = own.at[pl.ds(0, 2 * HALF * BLOCK)]
    pltpu.make_async_copy(sent, sent, send_far).wait()
    sent = picked.at[:, pl.ds(0, 2 * (HALF - 1))]
    pltpu.make_async_copy(sent, sent, send_in).wait()


def move_rows(tp_bits, stored, scale, slot_expert):
    rows = stored.shape[0]
    row_blocks = rows // BLOCK
    dma = pltpu.SemaphoreType.DMA
    return pl.pallas_call(
        functools.partial(move_kernel, tp_bits),
        out_shape=(
            jax.ShapeDtypeStruct((2, rows, BLOCK), jnp.bfloat16),
            jax.ShapeDtypeStruct((EP, 1, BLOCK), jnp.float32),
        ),
        in_specs=[
            pl.BlockSpec(memory_space=pltpu.SMEM),
            pl.BlockSpec(memory_space=pl.ANY),
            pl.BlockSpec(memory_space=pltpu.VMEM),
        ],
        out_specs=(pl.BlockSpec(memory_space=pl.ANY), pl.BlockSpec(memory_space=pl.ANY)),
        scratch_shapes=[
            pltpu.VMEM((rows, BLOCK), jnp.bfloat16),
            pltpu.VMEM((BLOCK, BLOCK), jnp.bfloat16),
            pltpu.VMEM((STAGES, 2 * HALF, 2, PIECE, BLOCK), jnp.bfloat16),
            pltpu.VMEM((row_blocks, BLOCK), jnp.float32),
            pltpu.VMEM((max(tp_bits, 1), 8, BLOCK), jnp.float32),
            pltpu.VMEM((max(tp_bits, 1), 8, BLOCK), jnp.float32),
            pltpu.VMEM((1, 1, BLOCK), jnp.float32),
            dma,
            dma((2, STAGES)),
            dma((2, STAGES)),
            dma((STAGES,)),
            dma,
            dma((max(tp_bits, 1),)),
            dma,
            dma,
            dma,
            dma,
            dma((max(tp_bits, 1),)),
        ]
        + [pltpu.VMEM((2 * HALF, PIECE, BLOCK), jnp.bfloat16)] * (2 * STAGES),
        compiler_params=pltpu.CompilerParams(collective_id=0, has_side_effects=True),
        name="move_rows",
    )(slot_expert, stored, scale)


TILE = 1024


def finish_kernel(slot_ref, raw_ref, table_ref, out_ref, largest_ref, signs, factors):
    slot, tile = pl.program_id(0), pl.program_id(1)
    row_blocks = factors.shape[0]
    blocks = TILE // BLOCK

    @pl.when((slot == 0) & (tile == 0))
    def _():
        signs[...] = sign_matrix()

    @pl.when(tile == 0)
    def _():
        expert = slot_ref[2 * lax.axis_index("ep") + slot]
        row = table_ref[expert]
        lane = lax.broadcasted_iota(jnp.int32, (1, BLOCK), 1)
        largest = jnp.max(jnp.where(lane < row_blocks, 0.0, row))
        largest_ref[slot] = largest
        bound = jnp.full((row_blocks, BLOCK), largest, jnp.float32) + EPSILON
        scale = jnp.broadcast_to(to_column(row, row_blocks), (row_blocks, BLOCK))
        factors[...] = (scale * (1.0 / math.sqrt(BLOCK))) / bound

    for block in range(blocks):
        at = pl.ds(block * BLOCK, BLOCK)
        turned = jnp.dot(raw_ref[0, at, :], signs[...], preferred_element_type=jnp.float32)
        factor = factors[pl.ds(tile * blocks + block, 1), :]
        out_ref[0, at, :] = (turned * factor).astype(jnp.bfloat16)


def finish(raw, table, slot_expert):
    count, rows, width = raw.shape
    return pl.pallas_call(
        finish_kernel,
        grid=(count, rows // TILE),
        out_shape=(
            jax.ShapeDtypeStruct(raw.shape, jnp.bfloat16),
            jax.ShapeDtypeStruct((count,), jnp.float32),
        ),
        in_specs=[
            pl.BlockSpec(memory_space=pltpu.SMEM),
            pl.BlockSpec((1, TILE, width), lambda i, j: (i, j, 0)),
            pl.BlockSpec(memory_space=pltpu.VMEM),
        ],
        out_specs=(
            pl.BlockSpec((1, TILE, width), lambda i, j: (i, j, 0)),
            pl.BlockSpec(memory_space=pltpu.SMEM),
        ),
        scratch_shapes=[
            pltpu.VMEM((BLOCK, BLOCK), jnp.bfloat16),
            pltpu.VMEM((rows // BLOCK, BLOCK), jnp.float32),
        ],
        name="finish",
    )(slot_expert, raw, table)


def on_device(tp_bits, quantized, block_scale, slot_expert):
    rows = quantized.shape[1]
    stored = quantized.reshape(rows, BLOCK)
    scale = block_scale.reshape(1, rows // BLOCK)
    raw, table = move_rows(tp_bits, stored, scale, slot_expert)
    return finish(raw, table, slot_expert)


def solution(mesh):
    tp_bits = mesh.shape["tp"].bit_length() - 1
    in_specs = (P("ep", None, "tp"), P("ep", None, "tp"), P())
    out_specs = (P("ep", None, "tp"), P("ep"))
    return jax.shard_map(
        functools.partial(on_device, tp_bits),
        mesh=mesh,
        in_specs=in_specs,
        out_specs=out_specs,
        check_vma=False,
    )
```

```python
import functools
import math

import jax
import jax.numpy as jnp
from jax import lax
from jax.experimental import pallas as pl
from jax.experimental.pallas import tpu as pltpu
from jax.sharding import PartitionSpec as P

MESH = pl.DeviceIdType.MESH
BLOCK = 128
EPSILON = 1e-06
NX, NY = 4, 8
EP = NX * NY
HOLD = 4
OUT = (NY - HOLD) // 2
LAST = HOLD - 1
STAGES = 4
PIECE = BLOCK // STAGES
HUB = 0
VMEM_LIMIT = 16 << 20


def sign_matrix():
    rows = lax.broadcasted_iota(jnp.int32, (BLOCK, BLOCK), 0)
    cols = lax.broadcasted_iota(jnp.int32, (BLOCK, BLOCK), 1)
    common = rows & cols
    common = common ^ (common >> 4)
    common = common ^ (common >> 2)
    common = common ^ (common >> 1)
    return (1 - 2 * (common & 1)).astype(jnp.float32).astype(jnp.bfloat16)


def to_column(row, count):
    spread = jnp.broadcast_to(row, (count, BLOCK))
    at_row = lax.broadcasted_iota(jnp.int32, (count, BLOCK), 0)
    at_lane = lax.broadcasted_iota(jnp.int32, (count, BLOCK), 1)
    return jnp.sum(jnp.where(at_row == at_lane, spread, 0.0), axis=1, keepdims=True)


def move_kernel(
    tp_size,
    slot_hbm,
    stored_ref,
    scale_hbm,
    raw_ref,
    rows_ref,
    slot_ref,
    scale_ref,
    own,
    signs,
    picked,
    block_max,
    row_out,
    gathered,
    hub_out,
    hub_in,
    table_out,
    table,
    own_sem,
    small_sem,
    near_sem,
    right_sem,
    left_sem,
    in_sem,
    gather_sem,
    hub_sem,
    row_sem,
    pass_sem,
    send_near,
    send_right,
    send_left,
    send_in,
    send_gather,
    send_hub,
    send_row,
    send_pass,
    ready,
    *held_refs,
):
    held = [held_refs[k * STAGES : (k + 1) * STAGES] for k in range(HOLD)]
    me = lax.axis_index("ep")
    tp = lax.axis_index("tp")
    here_y, here_x = me // NX, lax.rem(me, NX)
    row_blocks = stored_ref.shape[0] // BLOCK
    is_hub = here_x == HUB

    def device(dy, x):
        return lax.rem(here_y + (NY + dy), NY) * NX + x, tp

    def across(dx):
        return lax.rem(here_x + dx, NX)

    barrier = pltpu.get_barrier_semaphore()
    for dy in range(-OUT, OUT + 1):
        for x in range(NX):
            if x == HUB:
                continue

            def greet(dy=dy, x=x):
                pl.semaphore_signal(barrier, inc=1, device_id=device(dy, x), device_id_type=MESH)

            if dy == 0:
                pl.when(here_x != x)(greet)
            else:
                greet()

    own_copy = pltpu.make_async_copy(stored_ref, own, own_sem)
    own_copy.start()
    slot_copy = pltpu.make_async_copy(slot_hbm, slot_ref, small_sem.at[0])
    slot_copy.start()
    scale_copy = pltpu.make_async_copy(scale_hbm, scale_ref, small_sem.at[1])
    scale_copy.start()

    @pl.when(is_hub)
    def _():
        def greet(step, _):
            pl.semaphore_signal(
                barrier, inc=1, device_id=(me, lax.rem(tp + step, tp_size)), device_id_type=MESH
            )
            return _

        lax.fori_loop(1, tp_size, greet, 0)

    @pl.when(jnp.logical_not(is_hub))
    def _():
        pl.semaphore_wait(barrier, (2 * OUT + 1) * NX - 1)

    @pl.when(here_x == HUB + 1)
    def _():
        pl.semaphore_signal(ready, inc=1, device_id=device(0, HUB), device_id_type=MESH)

    @pl.when(is_hub)
    def _():
        pl.semaphore_wait(ready, 1)

    def near_copy(rel, dx, stage, local=False):
        k = min(max(rel, 0), LAST)
        dy = k - rel
        chunk = lax.rem(here_y + (2 * NY - rel), NY)
        to_x = across(dx)
        start = pl.multiple_of((chunk * NX + to_x) * BLOCK + stage * PIECE, PIECE)
        source = stored_ref.at[pl.ds(start, PIECE)]
        target = held[k][stage].at[(rel + OUT) * NX + here_x]
        if local:
            return pltpu.make_async_copy(source, target, near_sem.at[k, stage])
        return pltpu.make_async_remote_copy(
            src_ref=source,
            dst_ref=target,
            send_sem=send_near,
            recv_sem=near_sem.at[k, stage],
            device_id=device(dy, to_x),
            device_id_type=MESH,
        )

    outside = [rel for reach in range(OUT, 0, -1) for rel in (-reach, LAST + reach)]
    inside = list(range(HOLD))
    for stage in range(STAGES):

        def send_outside(dx, _, stage=stage):
            for rel in outside:
                near_copy(rel, dx, stage).start()
            return _

        def send_inside(dx, _, stage=stage):
            for rel in inside:
                near_copy(rel, dx, stage).start()
            return _

        lax.fori_loop(0, NX, send_outside, 0)
        lax.fori_loop(1, NX, send_inside, 0)
        for rel in inside:
            near_copy(rel, 0, stage, local=True).start()

    signs[...] = sign_matrix()
    own_copy.wait()
    slot_copy.wait()
    scale_copy.wait()

    def some_blocks(index, _):
        at = pl.multiple_of(index * 8, 8)
        rows = own[pl.ds(pl.multiple_of(at * BLOCK, 8 * BLOCK), 8 * BLOCK), :]
        turned = jnp.dot(rows, signs[...], preferred_element_type=jnp.float32)
        block_max[pl.ds(at, 8), :] = jnp.max(jnp.abs(turned).reshape(8, BLOCK, BLOCK), axis=1)
        return _

    lax.fori_loop(0, row_blocks // 8, some_blocks, 0)
    row_out[...] = jnp.zeros_like(row_out)
    row_out[0, :, 0:row_blocks] = scale_ref[...].astype(jnp.float32)
    scale_row = row_out[0, :, :]
    largest = jnp.max(block_max[...] * to_column(scale_row, row_blocks)) * (1.0 / math.sqrt(BLOCK))
    lane = lax.broadcasted_iota(jnp.int32, (1, BLOCK), 1)
    row_out[0, :, :] = jnp.where(lane < row_blocks, scale_row, largest)

    gather_copy = pltpu.make_async_remote_copy(
        src_ref=row_out.at[0],
        dst_ref=gathered.at[here_x],
        send_sem=send_gather,
        recv_sem=gather_sem,
        device_id=device(0, HUB),
        device_id_type=MESH,
    )

    @pl.when(is_hub)
    def _():
        pltpu.make_async_copy(row_out.at[0], gathered.at[here_x], gather_sem).start()

    @pl.when(jnp.logical_not(is_hub))
    def _():
        gather_copy.start()

    lane3 = lax.broadcasted_iota(jnp.int32, (NX, 1, BLOCK), 2)

    def meet_hubs():
        @pl.when(is_hub)
        def _():
            pl.semaphore_wait(barrier, tp_size - 1)
            pltpu.make_async_copy(gathered, gathered, gather_sem).wait()
            hub_out[...] = gathered[...]

            def send_hub_row(step, _):
                pltpu.make_async_remote_copy(
                    src_ref=hub_out,
                    dst_ref=hub_in.at[tp],
                    send_sem=send_hub,
                    recv_sem=hub_sem,
                    device_id=(me, lax.rem(tp + step, tp_size)),
                    device_id_type=MESH,
                ).start()
                return _

            lax.fori_loop(1, tp_size, send_hub_row, 0)
            pltpu.make_async_copy(hub_out, hub_in.at[tp], hub_sem).start()

    def own_rows(dy):
        return table.at[pl.ds(lax.rem(here_y + (NY + dy), NY) * NX, NX)]

    def spread_rows():
        @pl.when(is_hub)
        def _():
            pltpu.make_async_copy(hub_in, hub_in, hub_sem).wait()
            table_out[...] = jnp.where(lane3 < row_blocks, hub_out[...], jnp.max(hub_in[...], axis=0))
            pltpu.make_async_copy(table_out, own_rows(0), row_sem).start()
            for dy in range(-OUT, OUT + 1):

                def send_rows(dx, _, dy=dy):
                    pltpu.make_async_remote_copy(
                        src_ref=table_out,
                        dst_ref=own_rows(0),
                        send_sem=send_row.at[dy + OUT],
                        recv_sem=row_sem,
                        device_id=device(dy, across(dx)),
                        device_id_type=MESH,
                    ).start()
                    return _

                lax.fori_loop(1 if dy == 0 else 0, NX, send_rows, 0)

    passed = [(-OUT, step) for step in range(1, NY // 2 - OUT + 1)]
    passed += [(OUT, -step) for step in range(1, (NY - 1) // 2 - OUT + 1)]

    def pass_copy(dy, step):
        return pltpu.make_async_remote_copy(
            src_ref=own_rows(step),
            dst_ref=own_rows(step),
            send_sem=send_pass,
            recv_sem=pass_sem,
            device_id=device(dy, here_x),
            device_id_type=MESH,
        )

    def pass_rows():
        near = table.at[pl.ds(0, (2 * OUT + 1) * NX)]
        pltpu.make_async_copy(near, near, row_sem).wait()
        for dy, step in passed:
            pass_copy(dy, step).start()

    def right_copy(k, stage):
        part = pl.ds(0, (OUT + k + 1) * NX)
        return pltpu.make_async_remote_copy(
            src_ref=held[k][stage].at[part],
            dst_ref=held[k + 1][stage].at[part],
            send_sem=send_right.at[k, stage],
            recv_sem=right_sem.at[k + 1, stage],
            device_id=device(1, here_x),
            device_id_type=MESH,
        )

    def left_copy(k, stage):
        part = pl.ds((OUT + k) * NX, (NY - OUT - k) * NX)
        return pltpu.make_async_remote_copy(
            src_ref=held[k][stage].at[part],
            dst_ref=held[k - 1][stage].at[part],
            send_sem=send_left.at[k, stage],
            recv_sem=left_sem.at[k - 1, stage],
            device_id=device(-1, here_x),
            device_id_type=MESH,
        )

    waited = set()

    def wait_near(k, stage):
        if (k, stage) not in waited:
            waited.add((k, stage))
            rows = NX * (OUT + 1 if k in (0, LAST) else 1)
            part = held[k][stage].at[pl.ds(0, rows)]
            pltpu.make_async_copy(part, part, near_sem.at[k, stage]).wait()

    def relay(level, stage):
        k = level
        wait_near(k, stage)
        if level > 0:
            right_copy(k - 1, stage).wait_recv()
        right_copy(k, stage).start()
        k = LAST - level
        wait_near(k, stage)
        if level > 0:
            left_copy(k + 1, stage).wait_recv()
        left_copy(k, stage).start()

    serves = [pair for reach in range(OUT, 0, -1) for pair in ((0, -reach), (LAST, reach))]
    far_count = len(serves)
    serves += [(k, 0) for k in range(HOLD)]

    def in_rows(k, stage):
        chunk = lax.rem(here_y + NY - k, NY)
        start = pl.multiple_of((chunk * NX + here_x) * BLOCK + stage * PIECE, PIECE)
        return raw_ref.at[:, pl.ds(start, PIECE)]

    def serve(stage):
        right_copy(LAST - 1, stage).wait_recv()
        left_copy(1, stage).wait_recv()

        def pick(dx, _):
            for at, (k, dy) in enumerate(serves):
                target, _tp = device(dy, across(dx))
                for slot in range(2):
                    expert = slot_ref[2 * target + slot]
                    away = ((expert >> 2) + (NY + k + OUT) - here_y) & 7
                    index = away * NX + (expert & 3)
                    picked[stage, at * NX + dx, slot] = held[k][stage][index]
            return _

        lax.fori_loop(0, NX, pick, 0)

        def send_in_one(dx, _, pairs):
            for at, (k, dy) in pairs:
                pltpu.make_async_remote_copy(
                    src_ref=picked.at[stage, at * NX + dx],
                    dst_ref=in_rows(k, stage),
                    send_sem=send_in,
                    recv_sem=in_sem.at[stage],
                    device_id=device(dy, across(dx)),
                    device_id_type=MESH,
                ).start()
            return _

        pairs = list(enumerate(serves))
        lax.fori_loop(0, NX, functools.partial(send_in_one, pairs=pairs[:far_count]), 0)
        lax.fori_loop(1, NX, functools.partial(send_in_one, pairs=pairs[far_count:]), 0)
        for at, (k, _dy) in pairs[far_count:]:
            pltpu.make_async_copy(
                picked.at[stage, at * NX], in_rows(k, stage), in_sem.at[stage]
            ).start()

    for turn in range(STAGES + LAST):
        for level in range(LAST):
            if 0 <= turn - level < STAGES:
                relay(level, turn - level)
        if turn == 1:
            meet_hubs()
        if turn == LAST:
            spread_rows()
        if turn == STAGES + LAST - 1:
            pass_rows()
        if turn >= LAST:
            serve(turn - LAST)

    passing = table.at[pl.ds(0, len(passed) * NX)]
    pltpu.make_async_copy(passing, passing, pass_sem).wait()
    for slot in range(2):
        rows_ref[slot] = table[slot_ref[2 * me + slot]]
    for stage in range(STAGES):
        part = raw_ref.at[:, pl.ds(0, EP * PIECE)]
        pltpu.make_async_copy(part, part, in_sem.at[stage]).wait()
    remote = EP - HOLD
    sent = own.at[pl.ds(0, remote * BLOCK)]
    pltpu.make_async_copy(sent, sent, send_near).wait()
    for stage in range(STAGES):
        for level in range(LAST):
            right_copy(level, stage).wait_send()
            left_copy(LAST - level, stage).wait_send()
    sent = picked.at[:, pl.ds(0, remote)]
    pltpu.make_async_copy(sent, sent, send_in).wait()
    pltpu.make_async_copy(passing, passing, send_pass).wait()

    @pl.when(jnp.logical_not(is_hub))
    def _():
        gather_copy.wait_send()

    @pl.when(is_hub)
    def _():
        sent = hub_in.at[pl.ds(0, tp_size - 1)]
        pltpu.make_async_copy(sent, sent, send_hub).wait()
        for dy in range(-OUT, OUT + 1):
            sent = hub_in.at[pl.ds(0, NX - 1 if dy == 0 else NX)]
            pltpu.make_async_copy(sent, sent, send_row.at[dy + OUT]).wait()


def move_rows(tp_size, stored, scale, slot_expert):
    rows = stored.shape[0]
    row_blocks = rows // BLOCK
    dma = pltpu.SemaphoreType.DMA
    return pl.pallas_call(
        functools.partial(move_kernel, tp_size),
        out_shape=(
            jax.ShapeDtypeStruct((2, rows, BLOCK), jnp.bfloat16),
            jax.ShapeDtypeStruct((2, 1, BLOCK), jnp.float32),
        ),
        in_specs=[pl.BlockSpec(memory_space=pltpu.HBM)] * 3,
        out_specs=(
            pl.BlockSpec(memory_space=pl.ANY),
            pl.BlockSpec(memory_space=pltpu.VMEM),
        ),
        scratch_shapes=[
            pltpu.SMEM(slot_expert.shape, jnp.int32),
            pltpu.VMEM(scale.shape, jnp.bfloat16),
            pltpu.VMEM((rows, BLOCK), jnp.bfloat16),
            pltpu.VMEM((BLOCK, BLOCK), jnp.bfloat16),
            pltpu.VMEM((STAGES, EP, 2, PIECE, BLOCK), jnp.bfloat16),
            pltpu.VMEM((row_blocks, BLOCK), jnp.float32),
            pltpu.VMEM((1, 1, BLOCK), jnp.float32),
            pltpu.VMEM((NX, 1, BLOCK), jnp.float32),
            pltpu.VMEM((NX, 1, BLOCK), jnp.float32),
            pltpu.VMEM((tp_size, NX, 1, BLOCK), jnp.float32),
            pltpu.VMEM((NX, 1, BLOCK), jnp.float32),
            pltpu.VMEM((EP, 1, BLOCK), jnp.float32),
            dma,
            dma((2,)),
            dma((HOLD, STAGES)),
            dma((HOLD, STAGES)),
            dma((HOLD, STAGES)),
            dma((STAGES,)),
            dma,
            dma,
            dma,
            dma,
            dma,
            dma((HOLD, STAGES)),
            dma((HOLD, STAGES)),
            dma,
            dma,
            dma,
            dma((2 * OUT + 1,)),
            dma,
            pltpu.SemaphoreType.REGULAR,
        ]
        + [pltpu.VMEM((EP, PIECE, BLOCK), jnp.bfloat16)] * (HOLD * STAGES),
        compiler_params=pltpu.CompilerParams(
            collective_id=0, has_side_effects=True, vmem_limit_bytes=VMEM_LIMIT
        ),
        name="move_rows",
    )(*(pltpu.with_memory_space_constraint(a, pltpu.HBM) for a in (slot_expert, stored, scale)))


TILE = 1024


def finish_kernel(raw_ref, rows_ref, out_ref, largest_ref, staged, factors, sems):
    count, rows, _ = staged.shape
    row_blocks = rows // BLOCK
    blocks = TILE // BLOCK
    signs = sign_matrix()
    lane = lax.broadcasted_iota(jnp.int32, (1, BLOCK), 1)
    copies = []
    for slot in range(count):
        row = rows_ref[slot]
        largest = jnp.max(jnp.where(lane < row_blocks, 0.0, row))
        largest_ref[slot] = largest
        bound = jnp.full((row_blocks, BLOCK), largest, jnp.float32) + EPSILON
        scale = jnp.broadcast_to(to_column(row, row_blocks), (row_blocks, BLOCK))
        factors[slot] = (scale * (1.0 / math.sqrt(BLOCK))) / bound
        for tile in range(rows // TILE):
            at = pl.ds(tile * TILE, TILE)
            turned = jnp.dot(raw_ref[slot, at, :], signs, preferred_element_type=jnp.float32)
            factor = factors[slot, pl.ds(tile * blocks, blocks), :]
            scaled = turned.reshape(blocks, BLOCK, BLOCK) * factor[:, None, :]
            staged[slot, at, :] = scaled.reshape(TILE, BLOCK).astype(jnp.bfloat16)
            copy = pltpu.make_async_copy(
                staged.at[slot, at], out_ref.at[slot, at], sems.at[slot, tile]
            )
            copy.start()
            copies.append(copy)
    for copy in copies:
        copy.wait()


def finish(raw, rows):
    count, height, width = raw.shape
    return pl.pallas_call(
        finish_kernel,
        out_shape=(
            jax.ShapeDtypeStruct(raw.shape, jnp.bfloat16),
            jax.ShapeDtypeStruct((count,), jnp.float32),
        ),
        in_specs=[
            pl.BlockSpec(memory_space=pltpu.VMEM),
            pl.BlockSpec(memory_space=pltpu.VMEM),
        ],
        out_specs=(
            pl.BlockSpec(memory_space=pltpu.HBM),
            pl.BlockSpec(memory_space=pltpu.SMEM),
        ),
        scratch_shapes=[
            pltpu.VMEM(raw.shape, jnp.bfloat16),
            pltpu.VMEM((count, height // BLOCK, BLOCK), jnp.float32),
            pltpu.SemaphoreType.DMA((count, height // TILE)),
        ],
        compiler_params=pltpu.CompilerParams(vmem_limit_bytes=VMEM_LIMIT),
        name="finish",
    )(raw, rows)


def on_device(tp_size, quantized, block_scale, slot_expert):
    rows = quantized.shape[1]
    stored = quantized.reshape(rows, BLOCK)
    scale = block_scale.reshape(1, rows // BLOCK)
    raw, picked_rows = move_rows(tp_size, stored, scale, slot_expert)
    return finish(raw, picked_rows)


def solution(mesh):
    in_specs = (P("ep", None, "tp"), P("ep", None, "tp"), P())
    out_specs = (P("ep", None, "tp"), P("ep"))
    return jax.shard_map(
        functools.partial(on_device, mesh.shape["tp"]),
        mesh=mesh,
        in_specs=in_specs,
        out_specs=out_specs,
        check_vma=False,
    )
```

```python
import functools
import math

import jax
import jax.numpy as jnp
from jax import lax
from jax.experimental import pallas as pl
from jax.experimental.pallas import tpu as pltpu
from jax.sharding import PartitionSpec as P

MESH = pl.DeviceIdType.MESH
BLOCK = 128
EPSILON = 1e-06
NX, NY = 4, 8
EP = NX * NY
HOLD = 4
OUT = (NY - HOLD) // 2
LAST = HOLD - 1
PIECES = (32, 32, 32, 32)
SUBS = (1, 1, 1, 1)
STAGES = len(PIECES)
STEPS = tuple((stage, part) for stage in range(len(PIECES)) for part in range(SUBS[stage]))
STARTS = tuple(sum(PIECES[:stage]) for stage in range(STAGES))
HUB = 0
VMEM_LIMIT = 16 << 20


def sign_matrix():
    rows = lax.broadcasted_iota(jnp.int32, (BLOCK, BLOCK), 0)
    cols = lax.broadcasted_iota(jnp.int32, (BLOCK, BLOCK), 1)
    common = rows & cols
    common = common ^ (common >> 4)
    common = common ^ (common >> 2)
    common = common ^ (common >> 1)
    return (1 - 2 * (common & 1)).astype(jnp.float32).astype(jnp.bfloat16)


def to_column(row, count):
    spread = jnp.broadcast_to(row, (count, BLOCK))
    at_row = lax.broadcasted_iota(jnp.int32, (count, BLOCK), 0)
    at_lane = lax.broadcasted_iota(jnp.int32, (count, BLOCK), 1)
    return jnp.sum(jnp.where(at_row == at_lane, spread, 0.0), axis=1, keepdims=True)


def move_kernel(
    tp_size,
    slot_hbm,
    stored_ref,
    scale_hbm,
    raw_ref,
    rows_ref,
    slot_ref,
    scale_ref,
    own,
    signs,
    block_max,
    row_out,
    gathered,
    hub_out,
    hub_in,
    table_out,
    table,
    own_sem,
    small_sem,
    near_sem,
    right_sem,
    left_sem,
    in_sem,
    gather_sem,
    hub_sem,
    row_sem,
    pass_sem,
    send_near,
    send_right,
    send_left,
    send_in,
    send_gather,
    send_hub,
    send_row,
    send_pass,
    ready,
    *buffers,
):
    held = [buffers[k * STAGES : (k + 1) * STAGES] for k in range(HOLD)]
    picked = buffers[HOLD * STAGES :]
    me = lax.axis_index("ep")
    tp = lax.axis_index("tp")
    here_y, here_x = me // NX, lax.rem(me, NX)
    row_blocks = stored_ref.shape[0] // BLOCK
    is_hub = here_x == HUB

    def device(dy, x):
        return lax.rem(here_y + (NY + dy), NY) * NX + x, tp

    def across(dx):
        return lax.rem(here_x + dx, NX)

    barrier = pltpu.get_barrier_semaphore()
    for dy in range(-OUT, OUT + 1):
        for x in range(NX):
            if x == HUB:
                continue

            def greet(dy=dy, x=x):
                pl.semaphore_signal(barrier, inc=1, device_id=device(dy, x), device_id_type=MESH)

            if dy == 0:
                pl.when(here_x != x)(greet)
            else:
                greet()

    own_copy = pltpu.make_async_copy(stored_ref, own, own_sem)
    own_copy.start()
    slot_copy = pltpu.make_async_copy(slot_hbm, slot_ref, small_sem.at[0])
    slot_copy.start()
    scale_copy = pltpu.make_async_copy(scale_hbm, scale_ref, small_sem.at[1])
    scale_copy.start()

    @pl.when(is_hub)
    def _():
        def greet(step, _):
            pl.semaphore_signal(
                barrier, inc=1, device_id=(me, lax.rem(tp + step, tp_size)), device_id_type=MESH
            )
            return _

        lax.fori_loop(1, tp_size, greet, 0)

    @pl.when(jnp.logical_not(is_hub))
    def _():
        pl.semaphore_wait(barrier, (2 * OUT + 1) * NX - 1)

    @pl.when(here_x == HUB + 1)
    def _():
        pl.semaphore_signal(ready, inc=1, device_id=device(0, HUB), device_id_type=MESH)

    @pl.when(is_hub)
    def _():
        pl.semaphore_wait(ready, 1)

    def near_copy(rel, dx, stage, local=False):
        k = min(max(rel, 0), LAST)
        dy = k - rel
        chunk = lax.rem(here_y + (2 * NY - rel), NY)
        to_x = across(dx)
        start = pl.multiple_of((chunk * NX + to_x) * BLOCK + STARTS[stage], 16)
        source = stored_ref.at[pl.ds(start, PIECES[stage])]
        target = held[k][stage].at[(rel + OUT) * NX + here_x]
        if local:
            return pltpu.make_async_copy(source, target, near_sem.at[k, stage])
        return pltpu.make_async_remote_copy(
            src_ref=source,
            dst_ref=target,
            send_sem=send_near,
            recv_sem=near_sem.at[k, stage],
            device_id=device(dy, to_x),
            device_id_type=MESH,
        )

    outside = [rel for reach in range(OUT, 0, -1) for rel in (-reach, LAST + reach)]
    inside = list(range(HOLD))

    def send_near_to(rels, stage):
        def send(dx, _):
            for rel in rels:
                near_copy(rel, dx, stage).start()
            return _

        lax.fori_loop(1 if rels[0] in inside else 0, NX, send, 0)

    for stage in range(STAGES):
        send_near_to(outside, stage)
        send_near_to([0, LAST], stage)
        for rel in inside:
            near_copy(rel, 0, stage, local=True).start()
        if stage > 0:
            send_near_to(inside[1:-1], stage - 1)
    send_near_to(inside[1:-1], STAGES - 1)

    gather_copy = pltpu.make_async_remote_copy(
        src_ref=row_out.at[0],
        dst_ref=gathered.at[here_x],
        send_sem=send_gather,
        recv_sem=gather_sem,
        device_id=device(0, HUB),
        device_id_type=MESH,
    )

    def find_largest():
        signs[...] = sign_matrix()
        own_copy.wait()
        slot_copy.wait()
        scale_copy.wait()

        def some_blocks(index, _):
            at = pl.multiple_of(index * 8, 8)
            rows = own[pl.ds(pl.multiple_of(at * BLOCK, 8 * BLOCK), 8 * BLOCK), :]
            turned = jnp.dot(rows, signs[...], preferred_element_type=jnp.float32)
            block_max[pl.ds(at, 8), :] = jnp.max(jnp.abs(turned).reshape(8, BLOCK, BLOCK), axis=1)
            return _

        lax.fori_loop(0, row_blocks // 8, some_blocks, 0)
        row_out[...] = jnp.zeros_like(row_out)
        row_out[0, :, 0:row_blocks] = scale_ref[...].astype(jnp.float32)
        scale_row = row_out[0, :, :]
        largest = jnp.max(block_max[...] * to_column(scale_row, row_blocks)) * (1.0 / math.sqrt(BLOCK))
        lane = lax.broadcasted_iota(jnp.int32, (1, BLOCK), 1)
        row_out[0, :, :] = jnp.where(lane < row_blocks, scale_row, largest)

        @pl.when(is_hub)
        def _():
            pltpu.make_async_copy(row_out.at[0], gathered.at[here_x], gather_sem).start()

        @pl.when(jnp.logical_not(is_hub))
        def _():
            gather_copy.start()

    lane3 = lax.broadcasted_iota(jnp.int32, (NX, 1, BLOCK), 2)

    def meet_hubs():
        @pl.when(is_hub)
        def _():
            pl.semaphore_wait(barrier, tp_size - 1)
            pltpu.make_async_copy(gathered, gathered, gather_sem).wait()
            hub_out[...] = gathered[...]

            def send_hub_row(step, _):
                pltpu.make_async_remote_copy(
                    src_ref=hub_out,
                    dst_ref=hub_in.at[tp],
                    send_sem=send_hub,
                    recv_sem=hub_sem,
                    device_id=(me, lax.rem(tp + step, tp_size)),
                    device_id_type=MESH,
                ).start()
                return _

            lax.fori_loop(1, tp_size, send_hub_row, 0)
            pltpu.make_async_copy(hub_out, hub_in.at[tp], hub_sem).start()

    def own_rows(dy):
        return table.at[pl.ds(lax.rem(here_y + (NY + dy), NY) * NX, NX)]

    def spread_rows():
        @pl.when(is_hub)
        def _():
            pltpu.make_async_copy(hub_in, hub_in, hub_sem).wait()
            table_out[...] = jnp.where(lane3 < row_blocks, hub_out[...], jnp.max(hub_in[...], axis=0))
            pltpu.make_async_copy(table_out, own_rows(0), row_sem).start()
            for dy in range(-OUT, OUT + 1):

                def send_rows(dx, _, dy=dy):
                    pltpu.make_async_remote_copy(
                        src_ref=table_out,
                        dst_ref=own_rows(0),
                        send_sem=send_row.at[dy + OUT],
                        recv_sem=row_sem,
                        device_id=device(dy, across(dx)),
                        device_id_type=MESH,
                    ).start()
                    return _

                lax.fori_loop(1 if dy == 0 else 0, NX, send_rows, 0)

    passed = [(-OUT, step) for step in range(1, NY // 2 - OUT + 1)]
    passed += [(OUT, -step) for step in range(1, (NY - 1) // 2 - OUT + 1)]

    def pass_copy(dy, step):
        return pltpu.make_async_remote_copy(
            src_ref=own_rows(step),
            dst_ref=own_rows(step),
            send_sem=send_pass,
            recv_sem=pass_sem,
            device_id=device(dy, here_x),
            device_id_type=MESH,
        )

    def pass_rows():
        near = table.at[pl.ds(0, (2 * OUT + 1) * NX)]
        pltpu.make_async_copy(near, near, row_sem).wait()
        for dy, step in passed:
            pass_copy(dy, step).start()

    def relay_part(k, step, experts):
        stage, part = STEPS[step]
        height = PIECES[stage] // SUBS[stage]
        return held[k][stage].at[experts, pl.ds(part * height, height)]

    def right_copy(k, step):
        experts = pl.ds(0, (OUT + k + 1) * NX)
        return pltpu.make_async_remote_copy(
            src_ref=relay_part(k, step, experts),
            dst_ref=relay_part(k + 1, step, experts),
            send_sem=send_right.at[k, step],
            recv_sem=right_sem.at[k + 1, step],
            device_id=device(1, here_x),
            device_id_type=MESH,
        )

    def left_copy(k, step):
        experts = pl.ds((OUT + k) * NX, (NY - OUT - k) * NX)
        return pltpu.make_async_remote_copy(
            src_ref=relay_part(k, step, experts),
            dst_ref=relay_part(k - 1, step, experts),
            send_sem=send_left.at[k, step],
            recv_sem=left_sem.at[k - 1, step],
            device_id=device(-1, here_x),
            device_id_type=MESH,
        )

    waited = set()

    def wait_near(k, step):
        stage = STEPS[step][0]
        if (k, stage) not in waited:
            waited.add((k, stage))
            rows = NX * (OUT + 1 if k in (0, LAST) else 1)
            part = held[k][stage].at[pl.ds(0, rows)]
            pltpu.make_async_copy(part, part, near_sem.at[k, stage]).wait()

    def relay(level, step):
        k = level
        wait_near(k, step)
        if level > 0:
            right_copy(k - 1, step).wait_recv()
        right_copy(k, step).start()
        k = LAST - level
        wait_near(k, step)
        if level > 0:
            left_copy(k + 1, step).wait_recv()
        left_copy(k, step).start()

    serves = [pair for reach in range(OUT, 0, -1) for pair in ((0, -reach), (LAST, reach))]
    far_count = len(serves)
    serves += [(k, 0) for k in range(HOLD)]

    def in_rows(k, stage):
        chunk = lax.rem(here_y + NY - k, NY)
        start = pl.multiple_of((chunk * NX + here_x) * BLOCK + STARTS[stage], 16)
        return raw_ref.at[:, pl.ds(start, PIECES[stage])]

    def serve(stage, part):
        def pick(dx, _, pairs):
            for at, (k, dy) in pairs:
                target, _tp = device(dy, across(dx))
                for slot in range(2):
                    expert = slot_ref[2 * target + slot]
                    away = ((expert >> 2) + (NY + k + OUT) - here_y) & 7
                    index = away * NX + (expert & 3)
                    picked[stage][at * NX + dx, slot] = held[k][stage][index]
            return _

        def send_in_one(turn, _, pairs):
            dx = lax.rem(2 + 3 * turn, NX) if pairs[0][0] < far_count else turn
            for at, (k, dy) in pairs:
                pltpu.make_async_remote_copy(
                    src_ref=picked[stage].at[at * NX + dx],
                    dst_ref=in_rows(k, stage),
                    send_sem=send_in.at[stage],
                    recv_sem=in_sem.at[stage],
                    device_id=device(dy, across(dx)),
                    device_id_type=MESH,
                ).start()
            return _

        pairs = list(enumerate(serves))
        far, rest = pairs[:far_count], pairs[far_count:]
        far, rest = ((far + rest, rest), (far[:2], []), (far[2:] + rest, rest))[part]
        far = [pair for pair in far if pair not in rest]
        lax.fori_loop(0, NX, functools.partial(pick, pairs=far), 0)
        for first in range(0, len(far), 2):
            lax.fori_loop(0, NX, functools.partial(send_in_one, pairs=far[first : first + 2]), 0)
        if not rest:
            return
        lax.fori_loop(0, NX, functools.partial(pick, pairs=rest), 0)
        lax.fori_loop(1, NX, functools.partial(send_in_one, pairs=rest), 0)
        for at, (k, _dy) in pairs[far_count:]:
            pltpu.make_async_copy(
                picked[stage].at[at * NX], in_rows(k, stage), in_sem.at[stage]
            ).start()

    count = len(STEPS)
    held_back = []
    for turn in range(count + LAST):
        for level in range(LAST):
            if 0 <= turn - level < count:
                relay(level, turn - level)
        if turn == 0:
            find_largest()
        if turn == 2:
            meet_hubs()
        if turn == 4:
            spread_rows()
        if turn == count + LAST - 1:
            pass_rows()
        while held_back:
            serve(held_back.pop(), 2)
        if turn >= LAST:
            step = turn - LAST
            right_copy(LAST - 1, step).wait_recv()
            left_copy(1, step).wait_recv()
            stage, part = STEPS[step]
            if part == SUBS[stage] - 1:
                if stage < STAGES - 1:
                    serve(stage, 1)
                    held_back.append(stage)
                else:
                    serve(stage, 0)

    passing = table.at[pl.ds(0, len(passed) * NX)]
    pltpu.make_async_copy(passing, passing, pass_sem).wait()
    for slot in range(2):
        rows_ref[slot] = table[slot_ref[2 * me + slot]]
    for stage in range(STAGES):
        part = raw_ref.at[:, pl.ds(0, EP * PIECES[stage])]
        pltpu.make_async_copy(part, part, in_sem.at[stage]).wait()
    remote = EP - HOLD
    sent = own.at[pl.ds(0, remote * BLOCK)]
    pltpu.make_async_copy(sent, sent, send_near).wait()
    for step in range(count):
        for level in range(LAST):
            right_copy(level, step).wait_send()
            left_copy(LAST - level, step).wait_send()
    for stage in range(STAGES):
        sent = picked[stage].at[pl.ds(0, remote)]
        pltpu.make_async_copy(sent, sent, send_in.at[stage]).wait()
    pltpu.make_async_copy(passing, passing, send_pass).wait()

    @pl.when(jnp.logical_not(is_hub))
    def _():
        gather_copy.wait_send()

    @pl.when(is_hub)
    def _():
        sent = hub_in.at[pl.ds(0, tp_size - 1)]
        pltpu.make_async_copy(sent, sent, send_hub).wait()
        for dy in range(-OUT, OUT + 1):
            sent = hub_in.at[pl.ds(0, NX - 1 if dy == 0 else NX)]
            pltpu.make_async_copy(sent, sent, send_row.at[dy + OUT]).wait()


def move_rows(tp_size, stored, scale, slot_expert):
    rows = stored.shape[0]
    row_blocks = rows // BLOCK
    dma = pltpu.SemaphoreType.DMA
    return pl.pallas_call(
        functools.partial(move_kernel, tp_size),
        out_shape=(
            jax.ShapeDtypeStruct((2, rows, BLOCK), jnp.bfloat16),
            jax.ShapeDtypeStruct((2, 1, BLOCK), jnp.float32),
        ),
        in_specs=[pl.BlockSpec(memory_space=pltpu.HBM)] * 3,
        out_specs=(
            pl.BlockSpec(memory_space=pl.ANY),
            pl.BlockSpec(memory_space=pltpu.VMEM),
        ),
        scratch_shapes=[
            pltpu.SMEM(slot_expert.shape, jnp.int32),
            pltpu.VMEM(scale.shape, jnp.bfloat16),
            pltpu.VMEM((rows, BLOCK), jnp.bfloat16),
            pltpu.VMEM((BLOCK, BLOCK), jnp.bfloat16),
            pltpu.VMEM((row_blocks, BLOCK), jnp.float32),
            pltpu.VMEM((1, 1, BLOCK), jnp.float32),
            pltpu.VMEM((NX, 1, BLOCK), jnp.float32),
            pltpu.VMEM((NX, 1, BLOCK), jnp.float32),
            pltpu.VMEM((tp_size, NX, 1, BLOCK), jnp.float32),
            pltpu.VMEM((NX, 1, BLOCK), jnp.float32),
            pltpu.VMEM((EP, 1, BLOCK), jnp.float32),
            dma,
            dma((2,)),
            dma((HOLD, STAGES)),
            dma((HOLD, len(STEPS))),
            dma((HOLD, len(STEPS))),
            dma((STAGES,)),
            dma,
            dma,
            dma,
            dma,
            dma,
            dma((HOLD, len(STEPS))),
            dma((HOLD, len(STEPS))),
            dma((STAGES,)),
            dma,
            dma,
            dma((2 * OUT + 1,)),
            dma,
            pltpu.SemaphoreType.REGULAR,
        ]
        + [pltpu.VMEM((EP, piece, BLOCK), jnp.bfloat16) for piece in PIECES] * HOLD
        + [pltpu.VMEM((EP, 2, piece, BLOCK), jnp.bfloat16) for piece in PIECES],
        compiler_params=pltpu.CompilerParams(
            collective_id=0, has_side_effects=True, vmem_limit_bytes=VMEM_LIMIT
        ),
        name="move_rows",
    )(*(pltpu.with_memory_space_constraint(a, pltpu.HBM) for a in (slot_expert, stored, scale)))


TILE = 1024


def finish_kernel(raw_ref, rows_ref, out_ref, largest_ref, staged, factors, sems):
    count, rows, _ = staged.shape
    row_blocks = rows // BLOCK
    blocks = TILE // BLOCK
    signs = sign_matrix()
    lane = lax.broadcasted_iota(jnp.int32, (1, BLOCK), 1)
    copies = []
    for slot in range(count):
        row = rows_ref[slot]
        largest = jnp.max(jnp.where(lane < row_blocks, 0.0, row))
        largest_ref[slot] = largest
        bound = jnp.full((row_blocks, BLOCK), largest, jnp.float32) + EPSILON
        scale = jnp.broadcast_to(to_column(row, row_blocks), (row_blocks, BLOCK))
        factors[slot] = (scale * (1.0 / math.sqrt(BLOCK))) / bound
        for tile in range(rows // TILE):
            at = pl.ds(tile * TILE, TILE)
            turned = jnp.dot(raw_ref[slot, at, :], signs, preferred_element_type=jnp.float32)
            factor = factors[slot, pl.ds(tile * blocks, blocks), :]
            scaled = turned.reshape(blocks, BLOCK, BLOCK) * factor[:, None, :]
            staged[slot, at, :] = scaled.reshape(TILE, BLOCK).astype(jnp.bfloat16)
            copy = pltpu.make_async_copy(
                staged.at[slot, at], out_ref.at[slot, at], sems.at[slot, tile]
            )
            copy.start()
            copies.append(copy)
    for copy in copies:
        copy.wait()


def finish(raw, rows):
    count, height, width = raw.shape
    return pl.pallas_call(
        finish_kernel,
        out_shape=(
            jax.ShapeDtypeStruct(raw.shape, jnp.bfloat16),
            jax.ShapeDtypeStruct((count,), jnp.float32),
        ),
        in_specs=[
            pl.BlockSpec(memory_space=pltpu.VMEM),
            pl.BlockSpec(memory_space=pltpu.VMEM),
        ],
        out_specs=(
            pl.BlockSpec(memory_space=pltpu.HBM),
            pl.BlockSpec(memory_space=pltpu.SMEM),
        ),
        scratch_shapes=[
            pltpu.VMEM(raw.shape, jnp.bfloat16),
            pltpu.VMEM((count, height // BLOCK, BLOCK), jnp.float32),
            pltpu.SemaphoreType.DMA((count, height // TILE)),
        ],
        compiler_params=pltpu.CompilerParams(vmem_limit_bytes=VMEM_LIMIT),
        name="finish",
    )(raw, rows)


def on_device(tp_size, quantized, block_scale, slot_expert):
    rows = quantized.shape[1]
    stored = quantized.reshape(rows, BLOCK)
    scale = block_scale.reshape(1, rows // BLOCK)
    raw, picked_rows = move_rows(tp_size, stored, scale, slot_expert)
    return finish(raw, picked_rows)


def solution(mesh):
    in_specs = (P("ep", None, "tp"), P("ep", None, "tp"), P())
    out_specs = (P("ep", None, "tp"), P("ep"))
    return jax.shard_map(
        functools.partial(on_device, mesh.shape["tp"]),
        mesh=mesh,
        in_specs=in_specs,
        out_specs=out_specs,
        check_vma=False,
    )
```

```python
import functools
import math

import jax
import jax.numpy as jnp
from jax import lax
from jax.experimental import pallas as pl
from jax.experimental.pallas import tpu as pltpu
from jax.sharding import PartitionSpec as P

MESH = pl.DeviceIdType.MESH
BLOCK = 128
EPSILON = 1e-06
NX, NY = 4, 8
EP = NX * NY
HOLD = 4
OUT = (NY - HOLD) // 2
LAST = HOLD - 1
PIECES = (32, 32, 32, 32)
SUBS = (1, 1, 1, 1)
STAGES = len(PIECES)
STEPS = tuple((stage, part) for stage in range(len(PIECES)) for part in range(SUBS[stage]))
STARTS = tuple(sum(PIECES[:stage]) for stage in range(STAGES))
HUB = 0
HELPER = 1
VMEM_LIMIT = 16 << 20


def sign_matrix():
    rows = lax.broadcasted_iota(jnp.int32, (BLOCK, BLOCK), 0)
    cols = lax.broadcasted_iota(jnp.int32, (BLOCK, BLOCK), 1)
    common = rows & cols
    common = common ^ (common >> 4)
    common = common ^ (common >> 2)
    common = common ^ (common >> 1)
    return (1 - 2 * (common & 1)).astype(jnp.float32).astype(jnp.bfloat16)


def to_column(row, count):
    spread = jnp.broadcast_to(row, (count, BLOCK))
    at_row = lax.broadcasted_iota(jnp.int32, (count, BLOCK), 0)
    at_lane = lax.broadcasted_iota(jnp.int32, (count, BLOCK), 1)
    return jnp.sum(jnp.where(at_row == at_lane, spread, 0.0), axis=1, keepdims=True)


def move_kernel(
    tp_size,
    slot_hbm,
    stored_ref,
    scale_hbm,
    raw_ref,
    largest_ref,
    factors_ref,
    signs,
    slot_ref,
    scale_ref,
    own,
    block_max,
    row_out,
    top_out,
    gathered,
    hub_out,
    hub_in,
    plane_out,
    tops,
    table,
    own_sem,
    small_sem,
    near_sem,
    right_sem,
    left_sem,
    in_sem,
    gather_sem,
    hub_sem,
    row_sem,
    pass_sem,
    scale_sem,
    tops_sem,
    send_scale,
    send_top,
    send_near,
    send_right,
    send_left,
    send_in,
    send_gather,
    send_hub,
    send_row,
    send_pass,
    ready,
    *buffers,
):
    held = [buffers[k * STAGES : (k + 1) * STAGES] for k in range(HOLD)]
    picked = buffers[HOLD * STAGES :]
    me = lax.axis_index("ep")
    tp = lax.axis_index("tp")
    here_y, here_x = me // NX, lax.rem(me, NX)
    row_blocks = stored_ref.shape[0] // BLOCK
    is_hub = me == HUB

    def device(dy, x):
        return lax.rem(here_y + (NY + dy), NY) * NX + x, tp

    def across(dx):
        return lax.rem(here_x + dx, NX)

    barrier = pltpu.get_barrier_semaphore()
    hub_y = HUB // NX
    for dy in range(-OUT, OUT + 1):
        for dx in range(NX):
            if dy == 0 and dx == 0:
                continue
            target, _tp = device(dy, across(dx))

            @pl.when(jnp.logical_not(is_hub) & (target != HUB))
            def _(target=target):
                pl.semaphore_signal(barrier, inc=1, device_id=(target, tp), device_id_type=MESH)

    own_copy = pltpu.make_async_copy(stored_ref, own, own_sem)
    own_copy.start()
    slot_copy = pltpu.make_async_copy(slot_hbm, slot_ref, small_sem.at[0])
    slot_copy.start()
    scale_copy = pltpu.make_async_copy(scale_hbm, scale_ref, small_sem.at[1])
    scale_copy.start()

    @pl.when(is_hub)
    def _():
        def greet(step, _):
            pl.semaphore_signal(
                barrier, inc=1, device_id=(me, lax.rem(tp + step, tp_size)), device_id_type=MESH
            )
            return _

        lax.fori_loop(1, tp_size, greet, 0)

        def greet_plane(step, _):
            pl.semaphore_signal(
                barrier, inc=1, device_id=(lax.rem(me + step, EP), tp), device_id_type=MESH
            )
            return _

        lax.fori_loop(1, EP, greet_plane, 0)

    @pl.when(jnp.logical_not(is_hub))
    def _():
        away = lax.rem(here_y - hub_y + NY, NY)
        beyond = (away > OUT) & (away < NY - OUT)
        pl.semaphore_wait(barrier, (2 * OUT + 1) * NX - 1 + jnp.where(beyond, 1, 0))

    @pl.when(me == HELPER)
    def _():
        pl.semaphore_signal(ready, inc=1, device_id=(HUB, tp), device_id_type=MESH)

    @pl.when(is_hub)
    def _():
        pl.semaphore_wait(ready, 1)

    def near_copy(rel, dx, stage, local=False):
        k = min(max(rel, 0), LAST)
        dy = k - rel
        chunk = lax.rem(here_y + (2 * NY - rel), NY)
        to_x = across(dx)
        start = pl.multiple_of((chunk * NX + to_x) * BLOCK + STARTS[stage], 16)
        source = stored_ref.at[pl.ds(start, PIECES[stage])]
        target = held[k][stage].at[(rel + OUT) * NX + here_x]
        if local:
            return pltpu.make_async_copy(source, target, near_sem.at[k, stage])
        return pltpu.make_async_remote_copy(
            src_ref=source,
            dst_ref=target,
            send_sem=send_near,
            recv_sem=near_sem.at[k, stage],
            device_id=device(dy, to_x),
            device_id_type=MESH,
        )

    outside = [rel for reach in range(OUT, 0, -1) for rel in (-reach, LAST + reach)]
    inside = list(range(HOLD))

    def send_near_to(rels, stage):
        def send(dx, _):
            for rel in rels:
                near_copy(rel, dx, stage).start()
            return _

        lax.fori_loop(1 if rels[0] in inside else 0, NX, send, 0)

    for stage in range(STAGES):
        send_near_to(outside, stage)
        send_near_to([0, LAST], stage)
        for rel in inside:
            near_copy(rel, 0, stage, local=True).start()
        if stage > 0:
            send_near_to(inside[1:-1], stage - 1)
    send_near_to(inside[1:-1], STAGES - 1)

    gather_copy = pltpu.make_async_remote_copy(
        src_ref=top_out.at[0],
        dst_ref=gathered.at[me],
        send_sem=send_gather,
        recv_sem=gather_sem,
        device_id=(HUB, tp),
        device_id_type=MESH,
    )

    def scale_copy_to(dx):
        return pltpu.make_async_remote_copy(
            src_ref=row_out.at[0],
            dst_ref=table.at[me],
            send_sem=send_scale,
            recv_sem=scale_sem,
            device_id=device(0, across(dx)),
            device_id_type=MESH,
        )

    def find_largest():
        signs[...] = sign_matrix()
        own_copy.wait()
        slot_copy.wait()
        scale_copy.wait()

        def some_blocks(index, _):
            at = pl.multiple_of(index * 8, 8)
            rows = own[pl.ds(pl.multiple_of(at * BLOCK, 8 * BLOCK), 8 * BLOCK), :]
            turned = jnp.dot(rows, signs[...], preferred_element_type=jnp.float32)
            block_max[pl.ds(at, 8), :] = jnp.max(jnp.abs(turned).reshape(8, BLOCK, BLOCK), axis=1)
            return _

        lax.fori_loop(0, row_blocks // 8, some_blocks, 0)
        row_out[...] = jnp.zeros_like(row_out)
        row_out[0, :, 0:row_blocks] = scale_ref[...].astype(jnp.float32)
        scale_row = row_out[0, :, :]
        largest = jnp.max(block_max[...] * to_column(scale_row, row_blocks)) * (1.0 / math.sqrt(BLOCK))
        top_out[...] = jnp.full((1, 1, BLOCK), largest, jnp.float32)
        pltpu.make_async_copy(row_out.at[0], table.at[me], scale_sem).start()
        for dx in range(1, NX):
            scale_copy_to(dx).start()

        @pl.when(is_hub)
        def _():
            pltpu.make_async_copy(top_out.at[0], gathered.at[me], gather_sem).start()

        @pl.when(jnp.logical_not(is_hub))
        def _():
            gather_copy.start()

    def meet_hubs():
        @pl.when(is_hub)
        def _():
            pl.semaphore_wait(barrier, tp_size - 1)
            pltpu.make_async_copy(gathered, gathered, gather_sem).wait()
            experts = lax.broadcasted_iota(jnp.int32, (EP, 1, BLOCK), 0)
            lanes = lax.broadcasted_iota(jnp.int32, (EP, 1, BLOCK), 2)
            hub_out[0] = jnp.max(jnp.where(experts == lanes, gathered[...], 0.0), axis=0)

            def send_hub_row(step, _):
                pltpu.make_async_remote_copy(
                    src_ref=hub_out.at[0],
                    dst_ref=hub_in.at[tp],
                    send_sem=send_hub,
                    recv_sem=hub_sem,
                    device_id=(me, lax.rem(tp + step, tp_size)),
                    device_id_type=MESH,
                ).start()
                return _

            lax.fori_loop(1, tp_size, send_hub_row, 0)
            pltpu.make_async_copy(hub_out.at[0], hub_in.at[tp], hub_sem).start()

    def spread_tops():
        @pl.when(is_hub)
        def _():
            pltpu.make_async_copy(hub_in, hub_in, hub_sem).wait()
            plane_out[0] = jnp.max(hub_in[...], axis=0)
            pltpu.make_async_copy(plane_out.at[0], tops.at[0], tops_sem).start()

            def send_tops(step, _):
                pltpu.make_async_remote_copy(
                    src_ref=plane_out.at[0],
                    dst_ref=tops.at[0],
                    send_sem=send_top,
                    recv_sem=tops_sem,
                    device_id=(lax.rem(me + step, EP), tp),
                    device_id_type=MESH,
                ).start()
                return _

            lax.fori_loop(1, EP, send_tops, 0)

    def own_rows(dy):
        return table.at[pl.ds(lax.rem(here_y + (NY + dy), NY) * NX, NX)]

    reached = [dy for dy in range(-OUT, OUT + 1) if dy != 0]

    def spread_rows():
        pltpu.make_async_copy(own_rows(0), own_rows(0), scale_sem).wait()
        for dy in reached:
            pltpu.make_async_remote_copy(
                src_ref=own_rows(0),
                dst_ref=own_rows(0),
                send_sem=send_row,
                recv_sem=row_sem,
                device_id=device(dy, here_x),
                device_id_type=MESH,
            ).start()

    passed = [(-OUT, step) for step in range(1, NY // 2 - OUT + 1)]
    passed += [(OUT, -step) for step in range(1, (NY - 1) // 2 - OUT + 1)]

    def pass_copy(dy, step):
        return pltpu.make_async_remote_copy(
            src_ref=own_rows(step),
            dst_ref=own_rows(step),
            send_sem=send_pass,
            recv_sem=pass_sem,
            device_id=device(dy, here_x),
            device_id_type=MESH,
        )

    def pass_rows():
        near = table.at[pl.ds(0, len(reached) * NX)]
        pltpu.make_async_copy(near, near, row_sem).wait()
        for dy, step in passed:
            pass_copy(dy, step).start()

    def relay_part(k, step, experts):
        stage, part = STEPS[step]
        height = PIECES[stage] // SUBS[stage]
        return held[k][stage].at[experts, pl.ds(part * height, height)]

    def right_copy(k, step):
        experts = pl.ds(0, (OUT + k + 1) * NX)
        return pltpu.make_async_remote_copy(
            src_ref=relay_part(k, step, experts),
            dst_ref=relay_part(k + 1, step, experts),
            send_sem=send_right.at[k, step],
            recv_sem=right_sem.at[k + 1, step],
            device_id=device(1, here_x),
            device_id_type=MESH,
        )

    def left_copy(k, step):
        experts = pl.ds((OUT + k) * NX, (NY - OUT - k) * NX)
        return pltpu.make_async_remote_copy(
            src_ref=relay_part(k, step, experts),
            dst_ref=relay_part(k - 1, step, experts),
            send_sem=send_left.at[k, step],
            recv_sem=left_sem.at[k - 1, step],
            device_id=device(-1, here_x),
            device_id_type=MESH,
        )

    waited = set()

    def wait_near(k, step):
        stage = STEPS[step][0]
        if (k, stage) not in waited:
            waited.add((k, stage))
            rows = NX * (OUT + 1 if k in (0, LAST) else 1)
            part = held[k][stage].at[pl.ds(0, rows)]
            pltpu.make_async_copy(part, part, near_sem.at[k, stage]).wait()

    def relay(level, step):
        k = level
        wait_near(k, step)
        if level > 0:
            right_copy(k - 1, step).wait_recv()
        right_copy(k, step).start()
        k = LAST - level
        wait_near(k, step)
        if level > 0:
            left_copy(k + 1, step).wait_recv()
        left_copy(k, step).start()

    serves = [pair for reach in range(OUT, 0, -1) for pair in ((0, -reach), (LAST, reach))]
    far_count = len(serves)
    serves += [(k, 0) for k in range(HOLD)]

    def in_rows(k, stage):
        chunk = lax.rem(here_y + NY - k, NY)
        start = pl.multiple_of((chunk * NX + here_x) * BLOCK + STARTS[stage], 16)
        return raw_ref.at[:, pl.ds(start, PIECES[stage])]

    def serve(stage, part):
        def pick(dx, _, pairs):
            for at, (k, dy) in pairs:
                target, _tp = device(dy, across(dx))
                for slot in range(2):
                    expert = slot_ref[2 * target + slot]
                    away = ((expert >> 2) + (NY + k + OUT) - here_y) & 7
                    index = away * NX + (expert & 3)
                    picked[stage][at * NX + dx, slot] = held[k][stage][index]
            return _

        def send_in_one(turn, _, pairs):
            dx = lax.rem(2 + 3 * turn, NX) if pairs[0][0] < far_count else turn
            for at, (k, dy) in pairs:
                pltpu.make_async_remote_copy(
                    src_ref=picked[stage].at[at * NX + dx],
                    dst_ref=in_rows(k, stage),
                    send_sem=send_in.at[stage],
                    recv_sem=in_sem.at[stage],
                    device_id=device(dy, across(dx)),
                    device_id_type=MESH,
                ).start()
            return _

        pairs = list(enumerate(serves))
        groups = [pairs[first : first + 2] for first in range(0, far_count, 2)]
        groups = (groups, groups[:1], groups[1:])[part]
        for group in groups:
            lax.fori_loop(0, NX, functools.partial(pick, pairs=group), 0)
            lax.fori_loop(0, NX, functools.partial(send_in_one, pairs=group), 0)
        if part == 1:
            return
        rest = pairs[far_count:]
        lax.fori_loop(0, NX, functools.partial(pick, pairs=rest), 0)
        lax.fori_loop(1, NX, functools.partial(send_in_one, pairs=rest), 0)
        for at, (k, _dy) in pairs[far_count:]:
            pltpu.make_async_copy(
                picked[stage].at[at * NX], in_rows(k, stage), in_sem.at[stage]
            ).start()

    count = len(STEPS)
    held_back = []
    for turn in range(count + LAST):
        for level in range(LAST):
            if 0 <= turn - level < count:
                relay(level, turn - level)
        if turn == 0:
            find_largest()
        if turn == 2:
            meet_hubs()
        if turn == 3:
            spread_rows()
        if turn == 4:
            spread_tops()
        if turn == count + LAST - 1:
            pass_rows()
        while held_back:
            serve(held_back.pop(), 2)
        if turn >= LAST:
            step = turn - LAST
            right_copy(LAST - 1, step).wait_recv()
            left_copy(1, step).wait_recv()
            stage, part = STEPS[step]
            if part == SUBS[stage] - 1:
                if stage < STAGES - 1:
                    serve(stage, 1)
                    held_back.append(stage)
                else:
                    serve(stage, 0)

    passing = table.at[pl.ds(0, len(passed) * NX)]
    pltpu.make_async_copy(passing, passing, pass_sem).wait()
    pltpu.make_async_copy(tops, tops, tops_sem).wait()
    lane = lax.broadcasted_iota(jnp.int32, (1, BLOCK), 1)
    for slot in range(2):
        expert = slot_ref[2 * me + slot]
        largest = jnp.max(jnp.where(lane == expert, tops[0], 0.0))
        largest_ref[slot] = jnp.full((1, BLOCK), largest, jnp.float32)
        bound = jnp.full((row_blocks, BLOCK), largest, jnp.float32) + EPSILON
        scale = jnp.broadcast_to(to_column(table[expert], row_blocks), (row_blocks, BLOCK))
        factors_ref[slot] = (scale * (1.0 / math.sqrt(BLOCK))) / bound
    for stage in range(STAGES):
        part = raw_ref.at[:, pl.ds(0, EP * PIECES[stage])]
        pltpu.make_async_copy(part, part, in_sem.at[stage]).wait()
    remote = EP - HOLD
    sent = own.at[pl.ds(0, remote * BLOCK)]
    pltpu.make_async_copy(sent, sent, send_near).wait()
    for step in range(count):
        for level in range(LAST):
            right_copy(level, step).wait_send()
            left_copy(LAST - level, step).wait_send()
    for stage in range(STAGES):
        sent = picked[stage].at[pl.ds(0, remote)]
        pltpu.make_async_copy(sent, sent, send_in.at[stage]).wait()
    pltpu.make_async_copy(passing, passing, send_pass).wait()

    @pl.when(jnp.logical_not(is_hub))
    def _():
        gather_copy.wait_send()

    @pl.when(is_hub)
    def _():
        sent = hub_in.at[pl.ds(0, tp_size - 1)]
        pltpu.make_async_copy(sent, sent, send_hub).wait()
        sent = gathered.at[pl.ds(0, EP - 1)]
        pltpu.make_async_copy(sent, sent, send_top).wait()

    sent = table.at[pl.ds(0, NX - 1)]
    pltpu.make_async_copy(sent, sent, send_scale).wait()
    sent = table.at[pl.ds(0, len(reached) * NX)]
    pltpu.make_async_copy(sent, sent, send_row).wait()


def move_rows(tp_size, stored, scale, slot_expert):
    rows = stored.shape[0]
    row_blocks = rows // BLOCK
    dma = pltpu.SemaphoreType.DMA
    return pl.pallas_call(
        functools.partial(move_kernel, tp_size),
        out_shape=(
            jax.ShapeDtypeStruct((2, rows, BLOCK), jnp.bfloat16),
            jax.ShapeDtypeStruct((2, 1, BLOCK), jnp.float32),
            jax.ShapeDtypeStruct((2, row_blocks, BLOCK), jnp.float32),
            jax.ShapeDtypeStruct((BLOCK, BLOCK), jnp.bfloat16),
        ),
        in_specs=[pl.BlockSpec(memory_space=pltpu.HBM)] * 3,
        out_specs=(
            pl.BlockSpec(memory_space=pl.ANY),
            pl.BlockSpec(memory_space=pltpu.VMEM),
            pl.BlockSpec(memory_space=pltpu.VMEM),
            pl.BlockSpec(memory_space=pltpu.VMEM),
        ),
        scratch_shapes=[
            pltpu.SMEM(slot_expert.shape, jnp.int32),
            pltpu.VMEM(scale.shape, jnp.bfloat16),
            pltpu.VMEM((rows, BLOCK), jnp.bfloat16),
            pltpu.VMEM((row_blocks, BLOCK), jnp.float32),
            pltpu.VMEM((1, 1, BLOCK), jnp.float32),
            pltpu.VMEM((1, 1, BLOCK), jnp.float32),
            pltpu.VMEM((EP, 1, BLOCK), jnp.float32),
            pltpu.VMEM((1, 1, BLOCK), jnp.float32),
            pltpu.VMEM((tp_size, 1, BLOCK), jnp.float32),
            pltpu.VMEM((1, 1, BLOCK), jnp.float32),
            pltpu.VMEM((1, 1, BLOCK), jnp.float32),
            pltpu.VMEM((EP, 1, BLOCK), jnp.float32),
            dma,
            dma((2,)),
            dma((HOLD, STAGES)),
            dma((HOLD, len(STEPS))),
            dma((HOLD, len(STEPS))),
            dma((STAGES,)),
            dma,
            dma,
            dma,
            dma,
            dma,
            dma,
            dma,
            dma,
            dma,
            dma((HOLD, len(STEPS))),
            dma((HOLD, len(STEPS))),
            dma((STAGES,)),
            dma,
            dma,
            dma,
            dma,
            pltpu.SemaphoreType.REGULAR,
        ]
        + [pltpu.VMEM((EP, piece, BLOCK), jnp.bfloat16) for piece in PIECES] * HOLD
        + [pltpu.VMEM((EP, 2, piece, BLOCK), jnp.bfloat16) for piece in PIECES],
        compiler_params=pltpu.CompilerParams(
            collective_id=0, has_side_effects=True, vmem_limit_bytes=VMEM_LIMIT
        ),
        name="move_rows",
    )(*(pltpu.with_memory_space_constraint(a, pltpu.HBM) for a in (slot_expert, stored, scale)))


TILE = 1024


def finish_kernel(raw_ref, tops_ref, factors_ref, signs_ref, out_ref, largest_ref, staged, sems):
    count, rows, _ = staged.shape
    blocks = TILE // BLOCK
    copies = []
    for slot in range(count):
        for tile in range(rows // TILE):
            at = pl.ds(tile * TILE, TILE)
            turned = jnp.dot(
                raw_ref[slot, at, :], signs_ref[...], preferred_element_type=jnp.float32
            )
            factor = factors_ref[slot, pl.ds(tile * blocks, blocks), :]
            scaled = turned.reshape(blocks, BLOCK, BLOCK) * factor[:, None, :]
            staged[slot, at, :] = scaled.reshape(TILE, BLOCK).astype(jnp.bfloat16)
            copy = pltpu.make_async_copy(
                staged.at[slot, at], out_ref.at[slot, at], sems.at[slot, tile]
            )
            copy.start()
            copies.append(copy)
    for slot in range(count):
        largest_ref[slot] = jnp.max(tops_ref[slot])
    for copy in copies:
        copy.wait()


def finish(raw, tops, factors, signs):
    count, height, width = raw.shape
    return pl.pallas_call(
        finish_kernel,
        out_shape=(
            jax.ShapeDtypeStruct(raw.shape, jnp.bfloat16),
            jax.ShapeDtypeStruct((count,), jnp.float32),
        ),
        in_specs=[pl.BlockSpec(memory_space=pltpu.VMEM)] * 4,
        out_specs=(
            pl.BlockSpec(memory_space=pltpu.HBM),
            pl.BlockSpec(memory_space=pltpu.SMEM),
        ),
        scratch_shapes=[
            pltpu.VMEM(raw.shape, jnp.bfloat16),
            pltpu.SemaphoreType.DMA((count, height // TILE)),
        ],
        compiler_params=pltpu.CompilerParams(vmem_limit_bytes=VMEM_LIMIT),
        name="finish",
    )(raw, tops, factors, signs)


def on_device(tp_size, quantized, block_scale, slot_expert):
    rows = quantized.shape[1]
    stored = quantized.reshape(rows, BLOCK)
    scale = block_scale.reshape(1, rows // BLOCK)
    return finish(*move_rows(tp_size, stored, scale, slot_expert))


def solution(mesh):
    in_specs = (P("ep", None, "tp"), P("ep", None, "tp"), P())
    out_specs = (P("ep", None, "tp"), P("ep"))
    return jax.shard_map(
        functools.partial(on_device, mesh.shape["tp"]),
        mesh=mesh,
        in_specs=in_specs,
        out_specs=out_specs,
        check_vma=False,
    )
```

```python
import functools
import math

import jax
import jax.numpy as jnp
from jax import lax
from jax.experimental import pallas as pl
from jax.experimental.pallas import tpu as pltpu
from jax.sharding import PartitionSpec as P

MESH = pl.DeviceIdType.MESH
BLOCK = 128
EPSILON = 1e-06
NX, NY = 4, 8
EP = NX * NY
HOLD = 4
OUT = (NY - HOLD) // 2
LAST = HOLD - 1
PIECES = (32, 32, 32, 32)
SUBS = (1, 1, 1, 1)
STAGES = len(PIECES)
STEPS = tuple((stage, part) for stage in range(len(PIECES)) for part in range(SUBS[stage]))
STARTS = tuple(sum(PIECES[:stage]) for stage in range(STAGES))
HUB = 0
HELPER = 1
VMEM_LIMIT = 16 << 20


def sign_matrix():
    rows = lax.broadcasted_iota(jnp.int32, (BLOCK, BLOCK), 0)
    cols = lax.broadcasted_iota(jnp.int32, (BLOCK, BLOCK), 1)
    common = rows & cols
    common = common ^ (common >> 4)
    common = common ^ (common >> 2)
    common = common ^ (common >> 1)
    return (1 - 2 * (common & 1)).astype(jnp.float32).astype(jnp.bfloat16)


def to_column(row, count):
    spread = jnp.broadcast_to(row, (count, BLOCK))
    at_row = lax.broadcasted_iota(jnp.int32, (count, BLOCK), 0)
    at_lane = lax.broadcasted_iota(jnp.int32, (count, BLOCK), 1)
    return jnp.sum(jnp.where(at_row == at_lane, spread, 0.0), axis=1, keepdims=True)


def move_kernel(
    tp_size,
    slot_hbm,
    stored_ref,
    scale_hbm,
    raw_ref,
    largest_ref,
    factors_ref,
    signs,
    slot_ref,
    scale_ref,
    own,
    block_max,
    row_out,
    top_out,
    gathered,
    hub_out,
    hub_in,
    plane_out,
    tops,
    table,
    own_sem,
    small_sem,
    near_sem,
    right_sem,
    left_sem,
    in_sem,
    gather_sem,
    hub_sem,
    row_sem,
    pass_sem,
    scale_sem,
    tops_sem,
    send_scale,
    send_top,
    send_near,
    send_right,
    send_left,
    send_in,
    send_gather,
    send_hub,
    send_row,
    send_pass,
    ready,
    *buffers,
):
    held = [buffers[k * STAGES : (k + 1) * STAGES] for k in range(HOLD)]
    picked = buffers[HOLD * STAGES :]
    me = lax.axis_index("ep")
    tp = lax.axis_index("tp")
    here_y, here_x = me // NX, lax.rem(me, NX)
    row_blocks = stored_ref.shape[0] // BLOCK
    is_hub = me == HUB

    def device(dy, x):
        return lax.rem(here_y + (NY + dy), NY) * NX + x, tp

    def across(dx):
        return lax.rem(here_x + dx, NX)

    barrier = pltpu.get_barrier_semaphore()
    hub_y = HUB // NX
    for dy in range(-OUT, OUT + 1):
        for dx in range(NX):
            if dy == 0 and dx == 0:
                continue
            target, _tp = device(dy, across(dx))

            @pl.when(jnp.logical_not(is_hub) & (target != HUB))
            def _(target=target):
                pl.semaphore_signal(barrier, inc=1, device_id=(target, tp), device_id_type=MESH)

    own_copy = pltpu.make_async_copy(stored_ref, own, own_sem)
    own_copy.start()
    slot_copy = pltpu.make_async_copy(slot_hbm, slot_ref, small_sem.at[0])
    slot_copy.start()
    scale_copy = pltpu.make_async_copy(scale_hbm, scale_ref, small_sem.at[1])
    scale_copy.start()

    @pl.when(is_hub)
    def _():
        def greet(step, _):
            pl.semaphore_signal(
                barrier, inc=1, device_id=(me, lax.rem(tp + step, tp_size)), device_id_type=MESH
            )
            return _

        lax.fori_loop(1, tp_size, greet, 0)

        def greet_plane(step, _):
            pl.semaphore_signal(
                barrier, inc=1, device_id=(lax.rem(me + step, EP), tp), device_id_type=MESH
            )
            return _

        lax.fori_loop(1, EP, greet_plane, 0)

    @pl.when(jnp.logical_not(is_hub))
    def _():
        away = lax.rem(here_y - hub_y + NY, NY)
        beyond = (away > OUT) & (away < NY - OUT)
        pl.semaphore_wait(barrier, (2 * OUT + 1) * NX - 1 + jnp.where(beyond, 1, 0))

    @pl.when(me == HELPER)
    def _():
        pl.semaphore_signal(ready, inc=1, device_id=(HUB, tp), device_id_type=MESH)

    @pl.when(is_hub)
    def _():
        pl.semaphore_wait(ready, 1)

    def near_copy(rel, dx, stage, local=False):
        k = min(max(rel, 0), LAST)
        dy = k - rel
        chunk = lax.rem(here_y + (2 * NY - rel), NY)
        to_x = across(dx)
        start = pl.multiple_of((chunk * NX + to_x) * BLOCK + STARTS[stage], 16)
        source = stored_ref.at[pl.ds(start, PIECES[stage])]
        target = held[k][stage].at[(rel + OUT) * NX + here_x]
        if local:
            return pltpu.make_async_copy(source, target, near_sem.at[k, stage])
        return pltpu.make_async_remote_copy(
            src_ref=source,
            dst_ref=target,
            send_sem=send_near,
            recv_sem=near_sem.at[k, stage],
            device_id=device(dy, to_x),
            device_id_type=MESH,
        )

    outside = [rel for reach in range(OUT, 0, -1) for rel in (-reach, LAST + reach)]
    inside = list(range(HOLD))

    def send_near_to(rels, stage):
        def send(dx, _):
            for rel in rels:
                near_copy(rel, dx, stage).start()
            return _

        lax.fori_loop(1 if rels[0] in inside else 0, NX, send, 0)

    for stage in range(STAGES):
        send_near_to(outside, stage)
        send_near_to([0, LAST], stage)
        for rel in inside:
            near_copy(rel, 0, stage, local=True).start()
        if stage > 0:
            send_near_to(inside[1:-1], stage - 1)
    send_near_to(inside[1:-1], STAGES - 1)

    gather_copy = pltpu.make_async_remote_copy(
        src_ref=top_out.at[0],
        dst_ref=gathered.at[me],
        send_sem=send_gather,
        recv_sem=gather_sem,
        device_id=(HUB, tp),
        device_id_type=MESH,
    )

    def scale_copy_to(dx):
        return pltpu.make_async_remote_copy(
            src_ref=row_out.at[0],
            dst_ref=table.at[me],
            send_sem=send_scale,
            recv_sem=scale_sem,
            device_id=device(0, across(dx)),
            device_id_type=MESH,
        )

    def find_largest():
        signs[...] = sign_matrix()
        own_copy.wait()
        slot_copy.wait()
        scale_copy.wait()

        def some_blocks(index, _):
            at = pl.multiple_of(index * 8, 8)
            rows = own[pl.ds(pl.multiple_of(at * BLOCK, 8 * BLOCK), 8 * BLOCK), :]
            turned = jnp.dot(rows, signs[...], preferred_element_type=jnp.float32)
            block_max[pl.ds(at, 8), :] = jnp.max(jnp.abs(turned).reshape(8, BLOCK, BLOCK), axis=1)
            return _

        lax.fori_loop(0, row_blocks // 8, some_blocks, 0)
        row_out[...] = jnp.zeros_like(row_out)
        row_out[0, :, 0:row_blocks] = scale_ref[...].astype(jnp.float32)
        scale_row = row_out[0, :, :]
        largest = jnp.max(block_max[...] * to_column(scale_row, row_blocks)) * (1.0 / math.sqrt(BLOCK))
        top_out[...] = jnp.full((1, 1, BLOCK), largest, jnp.float32)
        pltpu.make_async_copy(row_out.at[0], table.at[me], scale_sem).start()
        for dx in range(1, NX):
            scale_copy_to(dx).start()

        @pl.when(is_hub)
        def _():
            pltpu.make_async_copy(top_out.at[0], gathered.at[me], gather_sem).start()

        @pl.when(jnp.logical_not(is_hub))
        def _():
            gather_copy.start()

    def meet_hubs():
        @pl.when(is_hub)
        def _():
            pl.semaphore_wait(barrier, tp_size - 1)
            pltpu.make_async_copy(gathered, gathered, gather_sem).wait()
            experts = lax.broadcasted_iota(jnp.int32, (EP, 1, BLOCK), 0)
            lanes = lax.broadcasted_iota(jnp.int32, (EP, 1, BLOCK), 2)
            hub_out[0] = jnp.max(jnp.where(experts == lanes, gathered[...], 0.0), axis=0)

            def send_hub_row(step, _):
                pltpu.make_async_remote_copy(
                    src_ref=hub_out.at[0],
                    dst_ref=hub_in.at[tp],
                    send_sem=send_hub,
                    recv_sem=hub_sem,
                    device_id=(me, lax.rem(tp + step, tp_size)),
                    device_id_type=MESH,
                ).start()
                return _

            lax.fori_loop(1, tp_size, send_hub_row, 0)
            pltpu.make_async_copy(hub_out.at[0], hub_in.at[tp], hub_sem).start()

    def spread_tops():
        @pl.when(is_hub)
        def _():
            pltpu.make_async_copy(hub_in, hub_in, hub_sem).wait()
            plane_out[0] = jnp.max(hub_in[...], axis=0)
            pltpu.make_async_copy(plane_out.at[0], tops.at[0], tops_sem).start()

            def send_tops(step, _):
                pltpu.make_async_remote_copy(
                    src_ref=plane_out.at[0],
                    dst_ref=tops.at[0],
                    send_sem=send_top,
                    recv_sem=tops_sem,
                    device_id=(lax.rem(me + step, EP), tp),
                    device_id_type=MESH,
                ).start()
                return _

            lax.fori_loop(1, EP, send_tops, 0)

    def own_rows(dy):
        return table.at[pl.ds(lax.rem(here_y + (NY + dy), NY) * NX, NX)]

    reached = [dy for dy in range(-OUT, OUT + 1) if dy != 0]

    def spread_rows():
        pltpu.make_async_copy(own_rows(0), own_rows(0), scale_sem).wait()
        for dy in reached:
            pltpu.make_async_remote_copy(
                src_ref=own_rows(0),
                dst_ref=own_rows(0),
                send_sem=send_row,
                recv_sem=row_sem,
                device_id=device(dy, here_x),
                device_id_type=MESH,
            ).start()

    passed = [(-OUT, step) for step in range(1, NY // 2 - OUT + 1)]
    passed += [(OUT, -step) for step in range(1, (NY - 1) // 2 - OUT + 1)]

    def pass_copy(dy, step):
        return pltpu.make_async_remote_copy(
            src_ref=own_rows(step),
            dst_ref=own_rows(step),
            send_sem=send_pass,
            recv_sem=pass_sem,
            device_id=device(dy, here_x),
            device_id_type=MESH,
        )

    def pass_rows():
        near = table.at[pl.ds(0, len(reached) * NX)]
        pltpu.make_async_copy(near, near, row_sem).wait()
        for dy, step in passed:
            pass_copy(dy, step).start()

    def relay_part(k, step, experts):
        stage, part = STEPS[step]
        height = PIECES[stage] // SUBS[stage]
        return held[k][stage].at[experts, pl.ds(part * height, height)]

    def right_copy(k, step):
        experts = pl.ds(0, (OUT + k + 1) * NX)
        return pltpu.make_async_remote_copy(
            src_ref=relay_part(k, step, experts),
            dst_ref=relay_part(k + 1, step, experts),
            send_sem=send_right.at[k, step],
            recv_sem=right_sem.at[k + 1, step],
            device_id=device(1, here_x),
            device_id_type=MESH,
        )

    def left_copy(k, step):
        experts = pl.ds((OUT + k) * NX, (NY - OUT - k) * NX)
        return pltpu.make_async_remote_copy(
            src_ref=relay_part(k, step, experts),
            dst_ref=relay_part(k - 1, step, experts),
            send_sem=send_left.at[k, step],
            recv_sem=left_sem.at[k - 1, step],
            device_id=device(-1, here_x),
            device_id_type=MESH,
        )

    waited = set()

    def wait_near(k, step):
        stage = STEPS[step][0]
        if (k, stage) not in waited:
            waited.add((k, stage))
            rows = NX * (OUT + 1 if k in (0, LAST) else 1)
            part = held[k][stage].at[pl.ds(0, rows)]
            pltpu.make_async_copy(part, part, near_sem.at[k, stage]).wait()

    def relay(level, step):
        k = level
        wait_near(k, step)
        if level > 0:
            right_copy(k - 1, step).wait_recv()
        right_copy(k, step).start()
        k = LAST - level
        wait_near(k, step)
        if level > 0:
            left_copy(k + 1, step).wait_recv()
        left_copy(k, step).start()

    serves = [pair for reach in range(OUT, 0, -1) for pair in ((0, -reach), (LAST, reach))]
    far_count = len(serves)
    serves += [(k, 0) for k in range(HOLD)]

    def in_rows(k, stage):
        chunk = lax.rem(here_y + NY - k, NY)
        start = pl.multiple_of((chunk * NX + here_x) * BLOCK + STARTS[stage], 16)
        return raw_ref.at[:, pl.ds(start, PIECES[stage])]

    def serve(stage, part):
        def pick(dx, _, pairs):
            for at, (k, dy) in pairs:
                target, _tp = device(dy, across(dx))
                for slot in range(2):
                    expert = slot_ref[2 * target + slot]
                    away = ((expert >> 2) + (NY + k + OUT) - here_y) & 7
                    index = away * NX + (expert & 3)
                    picked[stage][at * NX + dx, slot] = held[k][stage][index]
            return _

        def send_in_one(turn, _, pairs):
            dx = lax.rem(2 + 3 * turn, NX) if pairs[0][0] < far_count else turn
            for at, (k, dy) in pairs:
                pltpu.make_async_remote_copy(
                    src_ref=picked[stage].at[at * NX + dx],
                    dst_ref=in_rows(k, stage),
                    send_sem=send_in.at[stage],
                    recv_sem=in_sem.at[stage],
                    device_id=device(dy, across(dx)),
                    device_id_type=MESH,
                ).start()
            return _

        pairs = list(enumerate(serves))
        groups = [pairs[first : first + 2] for first in range(0, far_count, 2)]
        groups = (groups, groups[:1], groups[1:])[part]
        for group in groups:
            lax.fori_loop(0, NX, functools.partial(pick, pairs=group), 0)
            lax.fori_loop(0, NX, functools.partial(send_in_one, pairs=group), 0)
        if part == 1:
            return
        rest = pairs[far_count:]
        lax.fori_loop(0, NX, functools.partial(pick, pairs=rest), 0)
        lax.fori_loop(1, NX, functools.partial(send_in_one, pairs=rest), 0)
        for at, (k, _dy) in pairs[far_count:]:
            pltpu.make_async_copy(
                picked[stage].at[at * NX], in_rows(k, stage), in_sem.at[stage]
            ).start()

    count = len(STEPS)
    held_back = []
    for turn in range(count + LAST):
        for level in range(LAST):
            if 0 <= turn - level < count:
                relay(level, turn - level)
        if turn == 0:
            find_largest()
        if turn == 2:
            meet_hubs()
        if turn == 3:
            spread_rows()
        if turn == 4:
            spread_tops()
        if turn == count + LAST - 1:
            pass_rows()
        while held_back:
            serve(held_back.pop(), 0)
        if turn >= LAST:
            step = turn - LAST
            right_copy(LAST - 1, step).wait_recv()
            left_copy(1, step).wait_recv()
            stage, part = STEPS[step]
            if part == SUBS[stage] - 1:
                if stage < STAGES - 1:
                    held_back.append(stage)
                else:
                    serve(stage, 0)

    passing = table.at[pl.ds(0, len(passed) * NX)]
    pltpu.make_async_copy(passing, passing, pass_sem).wait()
    pltpu.make_async_copy(tops, tops, tops_sem).wait()
    lane = lax.broadcasted_iota(jnp.int32, (1, BLOCK), 1)
    for slot in range(2):
        expert = slot_ref[2 * me + slot]
        largest = jnp.max(jnp.where(lane == expert, tops[0], 0.0))
        largest_ref[slot] = jnp.full((1, BLOCK), largest, jnp.float32)
        bound = jnp.full((row_blocks, BLOCK), largest, jnp.float32) + EPSILON
        scale = jnp.broadcast_to(to_column(table[expert], row_blocks), (row_blocks, BLOCK))
        factors_ref[slot] = (scale * (1.0 / math.sqrt(BLOCK))) / bound
    for stage in range(STAGES):
        part = raw_ref.at[:, pl.ds(0, EP * PIECES[stage])]
        pltpu.make_async_copy(part, part, in_sem.at[stage]).wait()
    remote = EP - HOLD
    sent = own.at[pl.ds(0, remote * BLOCK)]
    pltpu.make_async_copy(sent, sent, send_near).wait()
    for step in range(count):
        for level in range(LAST):
            right_copy(level, step).wait_send()
            left_copy(LAST - level, step).wait_send()
    for stage in range(STAGES):
        sent = picked[stage].at[pl.ds(0, remote)]
        pltpu.make_async_copy(sent, sent, send_in.at[stage]).wait()
    pltpu.make_async_copy(passing, passing, send_pass).wait()

    @pl.when(jnp.logical_not(is_hub))
    def _():
        gather_copy.wait_send()

    @pl.when(is_hub)
    def _():
        sent = hub_in.at[pl.ds(0, tp_size - 1)]
        pltpu.make_async_copy(sent, sent, send_hub).wait()
        sent = gathered.at[pl.ds(0, EP - 1)]
        pltpu.make_async_copy(sent, sent, send_top).wait()

    sent = table.at[pl.ds(0, NX - 1)]
    pltpu.make_async_copy(sent, sent, send_scale).wait()
    sent = table.at[pl.ds(0, len(reached) * NX)]
    pltpu.make_async_copy(sent, sent, send_row).wait()


def move_rows(tp_size, stored, scale, slot_expert):
    rows = stored.shape[0]
    row_blocks = rows // BLOCK
    dma = pltpu.SemaphoreType.DMA
    return pl.pallas_call(
        functools.partial(move_kernel, tp_size),
        out_shape=(
            jax.ShapeDtypeStruct((2, rows, BLOCK), jnp.bfloat16),
            jax.ShapeDtypeStruct((2, 1, BLOCK), jnp.float32),
            jax.ShapeDtypeStruct((2, row_blocks, BLOCK), jnp.float32),
            jax.ShapeDtypeStruct((BLOCK, BLOCK), jnp.bfloat16),
        ),
        in_specs=[pl.BlockSpec(memory_space=pltpu.HBM)] * 3,
        out_specs=(
            pl.BlockSpec(memory_space=pl.ANY),
            pl.BlockSpec(memory_space=pltpu.VMEM),
            pl.BlockSpec(memory_space=pltpu.VMEM),
            pl.BlockSpec(memory_space=pltpu.VMEM),
        ),
        scratch_shapes=[
            pltpu.SMEM(slot_expert.shape, jnp.int32),
            pltpu.VMEM(scale.shape, jnp.bfloat16),
            pltpu.VMEM((rows, BLOCK), jnp.bfloat16),
            pltpu.VMEM((row_blocks, BLOCK), jnp.float32),
            pltpu.VMEM((1, 1, BLOCK), jnp.float32),
            pltpu.VMEM((1, 1, BLOCK), jnp.float32),
            pltpu.VMEM((EP, 1, BLOCK), jnp.float32),
            pltpu.VMEM((1, 1, BLOCK), jnp.float32),
            pltpu.VMEM((tp_size, 1, BLOCK), jnp.float32),
            pltpu.VMEM((1, 1, BLOCK), jnp.float32),
            pltpu.VMEM((1, 1, BLOCK), jnp.float32),
            pltpu.VMEM((EP, 1, BLOCK), jnp.float32),
            dma,
            dma((2,)),
            dma((HOLD, STAGES)),
            dma((HOLD, len(STEPS))),
            dma((HOLD, len(STEPS))),
            dma((STAGES,)),
            dma,
            dma,
            dma,
            dma,
            dma,
            dma,
            dma,
            dma,
            dma,
            dma((HOLD, len(STEPS))),
            dma((HOLD, len(STEPS))),
            dma((STAGES,)),
            dma,
            dma,
            dma,
            dma,
            pltpu.SemaphoreType.REGULAR,
        ]
        + [pltpu.VMEM((EP, piece, BLOCK), jnp.bfloat16) for piece in PIECES] * HOLD
        + [pltpu.VMEM((EP, 2, piece, BLOCK), jnp.bfloat16) for piece in PIECES],
        compiler_params=pltpu.CompilerParams(
            collective_id=0, has_side_effects=True, vmem_limit_bytes=VMEM_LIMIT
        ),
        name="move_rows",
    )(*(pltpu.with_memory_space_constraint(a, pltpu.HBM) for a in (slot_expert, stored, scale)))


TILE = 1024


def finish_kernel(raw_ref, tops_ref, factors_ref, signs_ref, out_ref, largest_ref, staged, sems):
    count, rows, _ = staged.shape
    blocks = TILE // BLOCK
    copies = []
    for slot in range(count):
        for tile in range(rows // TILE):
            at = pl.ds(tile * TILE, TILE)
            turned = jnp.dot(
                raw_ref[slot, at, :], signs_ref[...], preferred_element_type=jnp.float32
            )
            factor = factors_ref[slot, pl.ds(tile * blocks, blocks), :]
            scaled = turned.reshape(blocks, BLOCK, BLOCK) * factor[:, None, :]
            staged[slot, at, :] = scaled.reshape(TILE, BLOCK).astype(jnp.bfloat16)
            copy = pltpu.make_async_copy(
                staged.at[slot, at], out_ref.at[slot, at], sems.at[slot, tile]
            )
            copy.start()
            copies.append(copy)
    for slot in range(count):
        largest_ref[slot] = jnp.max(tops_ref[slot])
    for copy in copies:
        copy.wait()


def finish(raw, tops, factors, signs):
    count, height, width = raw.shape
    return pl.pallas_call(
        finish_kernel,
        out_shape=(
            jax.ShapeDtypeStruct(raw.shape, jnp.bfloat16),
            jax.ShapeDtypeStruct((count,), jnp.float32),
        ),
        in_specs=[pl.BlockSpec(memory_space=pltpu.VMEM)] * 4,
        out_specs=(
            pl.BlockSpec(memory_space=pltpu.HBM),
            pl.BlockSpec(memory_space=pltpu.SMEM),
        ),
        scratch_shapes=[
            pltpu.VMEM(raw.shape, jnp.bfloat16),
            pltpu.SemaphoreType.DMA((count, height // TILE)),
        ],
        compiler_params=pltpu.CompilerParams(vmem_limit_bytes=VMEM_LIMIT),
        name="finish",
    )(raw, tops, factors, signs)


def on_device(tp_size, quantized, block_scale, slot_expert):
    rows = quantized.shape[1]
    stored = quantized.reshape(rows, BLOCK)
    scale = block_scale.reshape(1, rows // BLOCK)
    return finish(*move_rows(tp_size, stored, scale, slot_expert))


def solution(mesh):
    in_specs = (P("ep", None, "tp"), P("ep", None, "tp"), P())
    out_specs = (P("ep", None, "tp"), P("ep"))
    return jax.shard_map(
        functools.partial(on_device, mesh.shape["tp"]),
        mesh=mesh,
        in_specs=in_specs,
        out_specs=out_specs,
        check_vma=False,
    )
```
